32 devices in a mesh: groups: 2 (over y), sec: 4 (over z), tile: 2 (over x), row: 2 (over core).
Axes of the slice: x: 2, y: 2, z: 4, core: 2. Of those that a mesh axis runs over, the one named last changes fastest.
Arguments:
- section_pixels: float32 [8, 512, 4096], P(('groups', 'sec'), ('tile', 'row')), parts along dimension 0, may hold values from -40 to 40
- jitter_index: int32 [8, 512], P(('groups', 'sec'), ('tile', 'row')), parts along dimension 0, may hold values from 0 to 7
- drift_list: int32 [8, 4, 8, 3], P(('groups', 'sec')), parts along dimension 0, may hold values from 0 to 31, as said below
- blend_weight: float32 [8, 4, 8], P(('groups', 'sec')), parts along dimension 0, may hold values from 0.5 to 2
- patch_col: int32 [4, 8], P(('tile', 'row'), 'groups'), parts along dimension 1, may hold values from 0 to 896
Outputs:
- jitter_phase: float32 [8, 512], P(('groups', 'sec'), ('tile', 'row')), parts along dimension 0
- surfaces: float32 [6, 4, 4, 128, 128], P('groups', ('tile', 'row'), 'sec'), parts along dimension 0
The draws below stay inside these ranges and needn't reach their ends.
There are 2 independent parts, one for each index of `groups`. The reference program is written for one: setup_inputs(seed, part) draws one part's arguments, and reference() takes and returns one part's arrays. A program takes and returns all parts, laid end to end along the dimension named above; each array names one. Nothing has to cross between parts.
Inputs may be any that keep to these rules, and one draw needn't show every extreme that they name: `drift_list`: entry [s, j, k] names a block of band j (distinct over k), the band that owns its target, and the target block. No band sends more than 2 blocks to one owner, and in every section one owner receives exactly 2 blocks from every band.
All inputs are finite; a program needn't handle non-finite values.
Results may differ from the reference program's by a relative error of at most 0.0065.
Values may be sent and summed in bfloat16 or wider, within the bound.
A program may use at most 64 MiB of HBM per device.

```python
import math
import jax
import jax.numpy as jnp
from jax import lax

W = 4096
SEG = 512
PATCH = 128
BLOCK = 128
JMAX = 8
OV = 8
CAP = 2
ROWS_DEV = 128
SECTIONS = 4
OWNERS = 4
ROWS = 512
NBLK = 32
N_SEC = 4


def coarse_delays(key):
    return jax.random.randint(jax.random.fold_in(key, 11), (SECTIONS, ROWS), 0, JMAX).astype(jnp.int32)


def draw_jitter_index(key, part):
    return coarse_delays(key)


def draw_section_pixels(key, part):
    delays = coarse_delays(key)
    span_cols = W + JMAX + 1
    shared = jax.random.normal(jax.random.fold_in(key, 21), (1, ROWS + 1, span_cols), jnp.float32)
    own_field = jax.random.normal(jax.random.fold_in(key, 22), (SECTIONS, ROWS + 1, span_cols), jnp.float32)
    field_sum = 0.3 * shared + own_field
    mixed = (field_sum[:, 1:] + field_sum[:, :-1]) * 0.7071
    fraction = jax.random.uniform(jax.random.fold_in(key, 23), (SECTIONS, ROWS, 1), jnp.float32)
    columns = jnp.arange(W, dtype=jnp.int32)[None, None, :] - delays[:, :, None] + JMAX
    first_pick = jnp.take_along_axis(mixed, columns, 2)
    second_pick = jnp.take_along_axis(mixed, columns + 1, 2)
    noise_part = jax.random.normal(jax.random.fold_in(key, 24), (SECTIONS, ROWS, W), jnp.float32)
    picture = (1.0 - fraction) * first_pick + fraction * second_pick + 0.3 * noise_part
    return jnp.clip(picture, -40.0, 40.0)


def draw_drift_list(key, part):
    slot_count = OWNERS * CAP

    def one_band(band_key, hot_owner):
        perm_key, source_key, target_key, order_key = jax.random.split(band_key, 4)
        ordering = jax.random.permutation(perm_key, slot_count)
        placing = jnp.argsort(ordering)
        slot_ids = jnp.arange(slot_count, dtype=jnp.int32)
        sort_keys = jnp.where(slot_ids // CAP == hot_owner, slot_ids % CAP - CAP, placing)
        chosen = jnp.argsort(sort_keys)[:OV]
        owner_ids = chosen // CAP
        source_ids = jax.random.permutation(source_key, NBLK)[:OV]
        target_ids = jax.random.randint(target_key, (OV,), 0, NBLK)
        listing = jnp.stack([source_ids, owner_ids, target_ids], 1)
        return listing[jax.random.permutation(order_key, OV)]

    def one_section(section_key):
        hot_owner = jax.random.randint(jax.random.fold_in(section_key, 1), (), 0, OWNERS)
        band_keys = jax.random.split(jax.random.fold_in(section_key, 2), OWNERS)
        return jax.vmap(one_band, in_axes=(0, None))(band_keys, hot_owner)
    section_keys = jax.random.split(jax.random.fold_in(key, 31), SECTIONS)
    return jax.vmap(one_section)(section_keys).astype(jnp.int32)


def with_ends(result, own_key, smallest, high):
    shape = result.shape
    index_at = [jax.random.randint(jax.random.fold_in(own_key, axis), (), 0, shape[axis]) for axis in range(len(shape))]
    result = result.at[tuple(index_at)].set(smallest)
    longest = shape.index(max(shape))
    index_at[longest] = (index_at[longest] + 1) % shape[longest]
    return result.at[tuple(index_at)].set(high)


def block_levels(stream_key, extent, cuts, smallest, top_value):
    loudness, own = 1.0, jax.random.fold_in(stream_key, 6)
    for axis_at, shards_of in cuts:
        heights = jnp.exp(jax.random.uniform(jax.random.fold_in(own, axis_at), (shards_of,), jnp.float32, smallest / len(cuts), top_value / len(cuts)))
        loudness = loudness * jnp.repeat(heights, extent[axis_at] // shards_of).reshape([-1 if axis == axis_at else 1 for axis in range(len(extent))])
    return loudness


def setup_inputs(seed: int = 0, part: int = 0) -> dict:
    keys = jax.random.split(jax.random.key(seed), 6)
    part_keys = jax.random.split(jax.random.fold_in(keys[5], part), 6)
    section_pixels = draw_section_pixels(jax.random.fold_in(jax.random.fold_in(keys[5], part), 71), part)
    jitter_index = draw_jitter_index(jax.random.fold_in(jax.random.fold_in(keys[5], part), 71), part)
    drift_list = draw_drift_list(jax.random.fold_in(jax.random.fold_in(keys[5], part), 71), part)
    blend_weight = jnp.clip(jnp.exp(math.log(2.0) - 1.3862944 * jax.random.uniform(part_keys[3], (SECTIONS, OWNERS, OV), jnp.float32) ** block_levels(part_keys[3], (SECTIONS, OWNERS, OV), ((0, 4),), -0.2, 0.2)), 0.5, 2.0)
    patch_col = with_ends(jax.random.randint(part_keys[4], (OWNERS, N_SEC), 0, W // N_SEC - PATCH + 1), jax.random.fold_in(part_keys[4], 1), 0, (W // N_SEC - PATCH + 1) - 1).astype(jnp.int32)
    return {"section_pixels": section_pixels, "jitter_index": jitter_index, "drift_list": drift_list, "blend_weight": blend_weight, "patch_col": patch_col}


def dft_tables(length):
    indices = jnp.arange(length, dtype=jnp.int32)
    products = indices[:, None] * indices[None, :] % length
    angles = products.astype(jnp.float32) * (2.0 * math.pi / length)
    return (jnp.cos(angles), jnp.sin(angles))

def align_rows(pixels, delays):
    row_width = pixels.shape[1]
    padded = jnp.pad(pixels, ((0, 0), (0, JMAX)))
    aligned = jnp.zeros_like(pixels)
    for shift_by in range(JMAX):
        aligned = aligned + jnp.where(delays[:, None] == shift_by, padded[:, shift_by:shift_by + row_width], 0.0)
    return aligned

def row_spectra(rows):
    row_count, row_width = rows.shape
    cosine_table, sine_table = dft_tables(SEG)
    dft_table = jnp.concatenate([cosine_table, -sine_table], 1)
    spectra = jnp.dot(rows.reshape(row_count * (row_width // SEG), SEG), dft_table, precision=lax.Precision.HIGHEST, preferred_element_type=jnp.float32)
    spectra = spectra.reshape(row_count, row_width // SEG, 2 * SEG)
    return (spectra[..., :SEG], spectra[..., SEG:])

def jitter_estimate(now_real, now_imag, before_real, before_imag):
    indices = jnp.arange(SEG, dtype=jnp.int32)
    weights = jnp.sin(indices.astype(jnp.float32) * (2.0 * math.pi / SEG))
    cross_term = now_imag * before_real - now_real * before_imag
    numerator = lax.optimization_barrier(jnp.mean(weights * cross_term, axis=(1, 2)))
    power_sum = 0.5 * (now_real * now_real + now_imag * now_imag + before_real * before_real + before_imag * before_imag)
    return numerator / (lax.optimization_barrier(jnp.mean(power_sum, axis=(1, 2))) + 1e-05)

def correct_rows(aligned, jitter):
    padded = jnp.pad(aligned, ((0, 0), (1, 1)))
    slopes = 0.5 * (padded[:, 2:] - padded[:, :-2])
    return (aligned - jitter[:, None] * slopes).astype(jnp.bfloat16)

def left_mul(matrix, batch):
    return jnp.einsum('ij,...jk->...ik', matrix, batch, precision=lax.Precision.HIGHEST)

def right_mul(batch, matrix):
    return jnp.einsum('...ij,jk->...ik', batch, matrix, precision=lax.Precision.HIGHEST)

def correlate(patches):
    side = patches.shape[-1]
    cosine_table, sine_table = dft_tables(side)
    values = patches.astype(jnp.float32)
    first_cos = right_mul(values, cosine_table)
    first_sin = right_mul(values, sine_table)
    freq_real = left_mul(cosine_table, first_cos) - left_mul(sine_table, first_sin)
    freq_imag = -(left_mul(sine_table, first_cos) + left_mul(cosine_table, first_sin))
    cross_real = freq_real[:-1] * freq_real[1:] + freq_imag[:-1] * freq_imag[1:]
    cross_imag = freq_imag[:-1] * freq_real[1:] - freq_real[:-1] * freq_imag[1:]
    magnitude = jnp.sqrt(cross_real * cross_real + cross_imag * cross_imag)
    damping = 0.5 * lax.optimization_barrier(jnp.mean(magnitude, axis=(-2, -1), keepdims=True)) + 1e-06
    scaled = 1.0 / (magnitude + damping)
    damped_real = cross_real * scaled
    damped_imag = cross_imag * scaled
    back_real = right_mul(damped_real, cosine_table) - right_mul(damped_imag, sine_table)
    back_imag = right_mul(damped_real, sine_table) + right_mul(damped_imag, cosine_table)
    return (left_mul(cosine_table, back_real) - left_mul(sine_table, back_imag)) / side

def prepare(inputs):
    pixels, delays = inputs
    aligned = align_rows(pixels, delays)
    now_real, now_imag = row_spectra(aligned)
    zero_row = jnp.zeros_like(now_real[:1])
    before_real = jnp.concatenate([zero_row, now_real[:-1]], 0)
    before_imag = jnp.concatenate([zero_row, now_imag[:-1]], 0)
    jitter = jitter_estimate(now_real, now_imag, before_real, before_imag)
    return (correct_rows(aligned, jitter), jitter)

def blend_section(inputs):
    corrected, drifts, weights = inputs
    band_rows = ROWS_DEV // BLOCK
    across = W // BLOCK
    blocks = corrected.reshape(OWNERS, band_rows, BLOCK, across, BLOCK).transpose(0, 1, 3, 2, 4)
    blocks = blocks.reshape(OWNERS * NBLK, BLOCK, BLOCK).astype(jnp.float32)
    source_index = (jnp.arange(OWNERS, dtype=jnp.int32)[:, None] * NBLK + drifts[:, :, 0]).reshape(-1)
    target_index = (drifts[:, :, 1] * NBLK + drifts[:, :, 2]).reshape(-1)
    mixing = (jnp.arange(OWNERS * NBLK, dtype=jnp.int32)[:, None] == target_index[None, :]).astype(jnp.float32)
    mixing = mixing * weights.reshape(-1)[None, :]
    incoming = jnp.einsum('nm,mxy->nxy', mixing, blocks[source_index], precision=lax.Precision.HIGHEST)
    merged = (blocks + incoming) / (1.0 + lax.optimization_barrier(jnp.sum(mixing, axis=1)))[:, None, None]
    merged = merged.reshape(OWNERS, band_rows, across, BLOCK, BLOCK).transpose(0, 1, 3, 2, 4)
    return merged.reshape(ROWS, W).astype(jnp.bfloat16)

def reference(section_pixels, jitter_index, drift_list, blend_weight, patch_col):
    corrected, jitter = lax.map(prepare, (section_pixels, jitter_index))
    montage = lax.map(blend_section, (corrected, drift_list, blend_weight))
    slab_width = W // N_SEC
    patch_rows = ROWS_DEV // PATCH
    bands = montage.reshape(SECTIONS, ROWS // PATCH, PATCH, W)

    def slab_surfaces(slab_index):
        starts = slab_index * slab_width + jnp.repeat(patch_col[:, slab_index], patch_rows)
        picked = jax.vmap(lambda one_band, start_col: lax.dynamic_slice_in_dim(one_band, start_col, PATCH, 2), in_axes=(1, 0), out_axes=1)(bands, starts)
        return correlate(picked)
    surfaces = lax.map(slab_surfaces, jnp.arange(N_SEC, dtype=jnp.int32))
    return (jitter, jnp.transpose(surfaces, (1, 2, 0, 3, 4)))
```

```python
import functools
import math

import jax
import jax.numpy as jnp
import numpy as np
from jax import lax
from jax.experimental import pallas as pl
from jax.experimental.pallas import tpu as pltpu
from jax.sharding import PartitionSpec as P

SEG = 512
PATCH = 128
BLOCK = 128
CAP = 2
LANES = 128
MESH = pl.DeviceIdType.MESH


def dft_tables(side):
    index = np.arange(side)
    angles = (index[:, None] * index[None, :] % side) * (2.0 * math.pi / side)
    cosine, sine = np.cos(angles), np.sin(angles)
    table = np.concatenate(
        [
            np.concatenate([cosine, sine], 1),
            np.concatenate([cosine, -sine], 1),
            np.concatenate([-sine, -cosine], 1),
        ],
        0,
    )
    high = table.astype(jnp.bfloat16)
    low = (table - high.astype(np.float64)).astype(jnp.bfloat16)
    return np.stack([high, low])


def dot(a, b):
    return jnp.dot(a, b, preferred_element_type=jnp.float32)


def split(a):
    high = a.astype(jnp.bfloat16)
    return high, (a - high.astype(jnp.float32)).astype(jnp.bfloat16)


def dot3(a, b):
    return dot(a[0], b[0]) + (dot(a[0], b[1]) + dot(a[1], b[0]))


def total(terms):
    terms = list(terms)
    while len(terms) > 1:
        terms = [
            terms[i] + terms[i + 1] if i + 1 < len(terms) else terms[i]
            for i in range(0, len(terms), 2)
        ]
    return terms[0]


def take(x, index):
    return jnp.take_along_axis(x, index, axis=1)


def row_chunks(row_count):
    cuts = [16] + list(range(32, row_count, 32)) + [row_count]
    return [(a, b) for a, b in zip(cuts[:-1], cuts[1:])] + [(0, 16)]


def load_pieces(row_count):
    cuts = [0, 32, 80, row_count - 8]
    return [(row_count - 8, row_count)] + [(a, b) for a, b in zip(cuts[:-1], cuts[1:])]


def forward(patch, tables):
    wide = tables[0, 0:PATCH, :], tables[1, 0:PATCH, :]
    square = tables[0, PATCH : 3 * PATCH, :], tables[1, PATCH : 3 * PATCH, :]
    first = dot(patch, wide[0]) + dot(patch, wide[1])
    stacked = jnp.concatenate([first[:, :PATCH], first[:, PATCH:]], 0)
    return dot3(square, split(stacked))


def surface(now, after, tables):
    wide = tables[0, 0:PATCH, :]
    square = tables[0, PATCH : 3 * PATCH, :]
    now_real, now_imag = now[0:PATCH], now[PATCH : 2 * PATCH]
    next_real, next_imag = after[0:PATCH], after[PATCH : 2 * PATCH]
    cross_real = now_real * next_real + now_imag * next_imag
    cross_imag = now_imag * next_real - now_real * next_imag
    magnitude = jnp.sqrt(cross_real * cross_real + cross_imag * cross_imag)
    mean = jnp.sum(jnp.sum(magnitude, axis=0, keepdims=True), axis=1, keepdims=True) * (
        1.0 / (PATCH * PATCH)
    )
    scaled = 1.0 / (magnitude + (0.5 * mean + 1e-06))
    damped = jnp.concatenate([cross_real * scaled, cross_imag * scaled], 1)
    back = dot(damped.astype(jnp.bfloat16), square)
    stacked = jnp.concatenate([back[:, :PATCH], back[:, PATCH:]], 0)
    return dot(wide, stacked.astype(jnp.bfloat16)) * (1.0 / PATCH)


def kernel(
    sizes,
    pixels,
    delays_hbm,
    drifts_hbm,
    weights_hbm,
    columns_hbm,
    tables_hbm,
    jitter_out,
    freq_out,
    early_out,
    tables,
    raw,
    delays,
    drifts,
    weights,
    columns,
    delay_rows,
    aligned,
    ahead,
    cross_sums,
    energies,
    jitter_rows,
    halo_out,
    halo_in,
    outbox,
    arrived,
    coefs,
    partial,
    patch_out,
    patch_in,
    freq,
    load_sem,
    table_sem,
    small_sem,
    halo_sem,
    block_send,
    block_recv,
    patch_send,
    patch_recv,
):
    sections, tiles, rows_axis, row_count, row_width, moves = sizes
    owners = tiles * rows_axis
    blocks = row_width // LANES
    per_seg = SEG // LANES
    segs = row_width // SEG
    slab_blocks = blocks // sections
    chunks = row_chunks(row_count)
    pieces = load_pieces(row_count)
    f32, bf16 = jnp.float32, jnp.bfloat16
    tile, row_at = lax.axis_index("tile"), lax.axis_index("row")
    me = tile * rows_axis + row_at
    section = lax.axis_index("sec")

    def band_device(band):
        return {"tile": band // rows_axis, "row": band % rows_axis}

    band_steps = [(t, r) for t in range(tiles) for r in range(rows_axis)][1:]
    band_steps.sort(key=lambda step: -min(step[0], tiles - step[0]))

    def slot_of(step):
        return step[0] * rows_axis + step[1] - 1

    def band_at(step):
        return (tile + step[0]) % tiles * rows_axis + (row_at + step[1]) % rows_axis

    def band_from(step):
        return (tile - step[0] + tiles) % tiles * rows_axis + (
            row_at - step[1] + rows_axis
        ) % rows_axis

    upper = 2 * section // sections
    targets = []
    for i in range(sections - 1):
        up = i + (i + sections - section) // sections
        down = sections - 1 - i
        down = down - 1 + (down + sections - section - 1) // sections
        targets.append(upper * up + (1 - upper) * down)
    targets.append(section)

    table_copy = pltpu.make_async_copy(tables_hbm, tables, table_sem)
    loads = [
        pltpu.make_async_copy(
            pixels.at[0, pl.ds(a, b - a)], raw.at[pl.ds(a, b - a)], load_sem.at[i]
        )
        for i, (a, b) in enumerate(pieces)
    ]
    small_copies = [
        pltpu.make_async_copy(source, target, small_sem.at[i])
        for i, (source, target) in enumerate(
            (
                (delays_hbm, delays),
                (drifts_hbm, drifts),
                (weights_hbm, weights),
                (columns_hbm, columns),
            )
        )
    ]
    small_copies[0].start()
    for copy in loads[:2]:
        copy.start()
    for copy in small_copies[1:]:
        copy.start()
    for copy in loads[2:]:
        copy.start()
    table_copy.start()

    barrier = pltpu.get_barrier_semaphore()
    for step in range(1, owners):
        pl.semaphore_signal(
            barrier, inc=1, device_id=band_device((me + step) % owners), device_id_type=MESH
        )
    for step in range(1, sections):
        pl.semaphore_signal(
            barrier, inc=1, device_id={"sec": (section + step) % sections}, device_id_type=MESH
        )

    lane = lax.broadcasted_iota(jnp.int32, (8, LANES), 1)
    first_lane, last_lane = lane == 0, lane == LANES - 1
    to_right, to_left = (lane + 1) & (LANES - 1), (lane + LANES - 1) & (LANES - 1)
    zero = jnp.zeros((8, LANES), f32)
    for g in range(0, row_count + 8, 8):
        aligned[0, g : g + 8, :] = zero
        aligned[blocks + 1, g : g + 8, :] = zero
    small_copies[0].wait()
    delay_rows[...] = (
        jnp.broadcast_to(delays[...].astype(f32), (LANES, row_count)).T
    ).astype(jnp.int32)

    def shifted(g):
        start = g * 8
        delay = delay_rows[start : start + 8, :]
        values = [raw[start : start + 8, v * LANES : (v + 1) * LANES] for v in range(blocks)]
        near = lane + delay
        here = [take(x, near & (LANES - 1)) for x in values] + [zero]
        far = near + 1
        there = [take(x, far & (LANES - 1)) for x in values] + [zero]
        near_kept, far_kept = near < LANES, far < LANES
        now, after = [], []
        for v in range(blocks):
            now.append(jnp.where(near_kept, here[v], here[v + 1]))
            x = jnp.where(far_kept, there[v], there[v + 1])
            if v % per_seg == per_seg - 1:
                x = jnp.where(last_lane, there[v + 1 - per_seg], x)
            after.append(x)
        return now, after

    def keep(g, now, after):
        rows = slice(g * 8 + 8, g * 8 + 16)
        for v in range(blocks):
            aligned[v + 1, rows, :] = now[v]
            ahead[v, rows, :] = after[v]
        energies[rows, :] = total(x * x for x in now)

    def compare(g, now=None, after=None):
        start = g * 8
        terms = []
        for v in range(blocks):
            x = now[v] if now else aligned[v + 1, start + 8 : start + 16, :]
            x_after = after[v] if after else ahead[v, start + 8 : start + 16, :]
            above = aligned[v + 1, start + 7 : start + 15, :]
            above_after = ahead[v, start + 7 : start + 15, :]
            terms.append(above * x_after - above_after * x)
        cross_sums[start : start + 8, :] = total(terms)

    halo = pltpu.make_async_remote_copy(
        src_ref=halo_out.at[:, pl.ds(7, 1)],
        dst_ref=halo_in,
        send_sem=halo_sem.at[0],
        recv_sem=halo_sem.at[1],
        device_id=band_device((me + 1) % owners),
        device_id_type=MESH,
    )
    for copy in small_copies[1:]:
        copy.wait()

    def pick(hits, values, default):
        first = second = default
        for hit, value in zip(hits[::-1], values[::-1]):
            second = jnp.where(hit, first, second)
            first = jnp.where(hit, value, first)
        return first, second

    own_sources = [drifts[0, 0, me, k] for k in range(moves)]
    own_owners = [drifts[0, 1, me, k] for k in range(moves)]
    sources = {}
    for step in band_steps + [(0, 0)]:
        owner = band_at(step)
        picked = pick([o == owner for o in own_owners], own_sources, jnp.int32(0))
        for rank in range(CAP):
            sources[step, rank] = picked[rank]

    def corrected(block, start):
        rows = slice(start + 8, start + 16)
        before, x, after = [aligned[block + i, rows, :] for i in range(3)]
        left = take(jnp.where(last_lane, before, x), to_left)
        right = take(jnp.where(first_lane, after, x), to_right)
        return x - jitter_rows[start : start + 8, :] * (right - left)

    def finish(a, b):
        numerator = jnp.sum(cross_sums[a:b, :], axis=1, keepdims=True) * (-0.5 / segs)
        power = energies[a + 8 : b + 8, :] + energies[a + 7 : b + 7, :]
        power = jnp.sum(power, axis=1, keepdims=True) * (0.5 / segs)
        jitter = jnp.broadcast_to(numerator / (power + 1e-05), (b - a, LANES))
        jitter_rows[a:b, :] = 0.5 * jitter

    def fill_blocks(c):
        a, b = chunks[c]
        for step in band_steps:
            for rank in range(CAP):
                for start in range(a, b, 16):
                    pair = [corrected(sources[step, rank], start + i) for i in (0, 8)]
                    outbox[slot_of(step), rank, start : start + 16, :] = jnp.concatenate(
                        pair, 0
                    ).astype(bf16)

    def send_blocks(c):
        a, b = chunks[c]
        for step in band_steps:
            slot = slot_of(step)
            copy = pltpu.make_async_remote_copy(
                src_ref=outbox.at[slot, :, pl.ds(a, b - a)],
                dst_ref=arrived.at[slot, :, pl.ds(a, b - a)],
                send_sem=block_send,
                recv_sem=block_recv.at[c],
                device_id=band_device(band_at(step)),
                device_id_type=MESH,
            )
            copy.start()

    steps = [(0, 0)] + band_steps
    keys = [(step, rank) for step in steps for rank in range(CAP)]

    offsets = [columns[0, target] for target in targets]
    blocks_at = [t * slab_blocks + o // LANES for t, o in zip(targets, offsets)]
    starts = [o % LANES for o in offsets]

    def weigh():
        found = {}
        for step in steps:
            band = band_from(step)
            hits = [drifts[0, 1, band, k] == me for k in range(moves)]
            picked = pick(hits, [drifts[0, 2, band, k] for k in range(moves)], jnp.int32(-1))
            heavy = pick(hits, [weights[0, band, k] for k in range(moves)], jnp.float32(0.0))
            for rank in range(CAP):
                found[step, rank] = picked[rank], heavy[rank]
        for p in range(sections):
            under = jnp.where(lane >= starts[p], blocks_at[p], blocks_at[p] + 1)
            shares = [jnp.where(under == found[key][0], found[key][1], 0.0) for key in keys]
            scale = 1.0 / (1.0 + total(shares))
            coefs[p, len(keys)] = scale
            for i, share in enumerate(shares):
                coefs[p, i] = share * scale

    def own_part(a, b):
        for start in range(a, b, 8):
            rows = slice(start + 8, start + 16)
            half = jitter_rows[start : start + 8, :]
            mine = [
                corrected(sources[(0, 0), rank], start).astype(bf16).astype(f32)
                for rank in range(CAP)
            ]
            for p in range(sections):
                block, offset = blocks_at[p], starts[p]
                before, x, after = [aligned[block + i, rows, :] for i in range(3)]
                left = jnp.where(lane >= offset - 1, x, after)
                left = jnp.where((lane - offset) == LANES - 1, before, left)
                left = take(left, to_left)
                right = take(jnp.where(lane > offset, x, after), to_right)
                value = jnp.where(lane >= offset, x, after) - half * (right - left)
                value = value.astype(bf16).astype(f32) * coefs[p, len(keys)]
                for rank in range(CAP):
                    value = value + coefs[p, rank] * mine[rank]
                partial[p, start : start + 8, :] = value

    def send_patches(c):
        a, b = chunks[c]
        pltpu.make_async_copy(
            arrived.at[:, :, pl.ds(a, b - a)], arrived.at[:, :, pl.ds(a, b - a)], block_recv.at[c]
        ).wait()
        for start in range(a, b, 16):
            blocks_in = [
                arrived[slot_of(step), rank, start : start + 16, :].astype(f32)
                for step, rank in keys[CAP:]
            ]
            for p in range(sections):
                turn = (lane + starts[p]) & (LANES - 1)
                shares = [coefs[p, CAP + i] for i in range(len(blocks_in))]
                values = []
                for i in (0, 8):
                    terms = [share * x[i : i + 8] for share, x in zip(shares, blocks_in)]
                    values.append(take(partial[p, start + i : start + i + 8, :] + total(terms), turn))
                patch = jnp.concatenate(values, 0).astype(bf16)
                if p < sections - 1:
                    patch_out[p, start : start + 16, :] = patch
                else:
                    patch_in[section, start : start + 16, :] = patch
        for p, target in enumerate(targets[:-1]):
            pltpu.make_async_remote_copy(
                src_ref=patch_out.at[p, pl.ds(a, b - a)],
                dst_ref=patch_in.at[section, pl.ds(a, b - a)],
                send_sem=patch_send,
                recv_sem=patch_recv.at[section],
                device_id={"sec": target},
                device_id_type=MESH,
            ).start()

    last_group = row_count // 8 - 1

    def group(g):
        if g == last_group:
            compare(g)
            return
        now, after = shifted(g)
        keep(g, now, after)
        compare(g, now, after)

    loads[0].wait()
    loads[1].wait()
    keep(last_group, *shifted(last_group))
    for v in range(blocks):
        halo_out[v, :, :] = aligned[v + 1, row_count : row_count + 8, :]
    keep(1, *shifted(1))
    for c, (a, b) in enumerate(chunks[:-1]):
        if c == 1:
            for load in loads[2:]:
                load.wait()
        for g in range(a // 8, b // 8):
            group(g)
        finish(a, b)
        fill_blocks(c)
        if c == 0:
            pl.semaphore_wait(barrier, owners + sections - 2)
            halo.start()
        send_blocks(c)

    keep(0, *shifted(0))
    compare(1)
    halo.wait_recv()
    shown = jnp.where(me == 0, 0.0, 1.0)
    above = [shown * jnp.broadcast_to(halo_in[v], (8, LANES)) for v in range(blocks)]
    turned = [take(x, to_right) for x in above]
    for v in range(blocks):
        follows = v + 1 - per_seg if v % per_seg == per_seg - 1 else v + 1
        aligned[v + 1, 0:8, :] = above[v]
        ahead[v, 0:8, :] = jnp.where(last_lane, turned[follows], turned[v])
    energies[0:8, :] = total(x * x for x in above)
    compare(0)
    finish(*chunks[-1])
    fill_blocks(len(chunks) - 1)
    send_blocks(len(chunks) - 1)
    weigh()
    for a, b in chunks:
        own_part(a, b)
    for c in range(len(chunks)):
        send_patches(c)

    jitter_out[...] = 2.0 * jitter_rows[...].T[0:1, :]
    table_copy.wait()
    for s in range(sections):

        @pl.when(section != s)
        def _():
            pltpu.make_async_copy(patch_in.at[s], patch_in.at[s], patch_recv.at[s]).wait()

        if s < sections - 2:
            freq[s] = forward(patch_in[s], tables)
        else:
            freq_out[s - sections + 2] = forward(patch_in[s], tables)
        if 0 < s < sections - 1:
            after = freq[s] if s < sections - 2 else freq_out[0]
            early_out[s - 1] = surface(freq[s - 1], after, tables)

    halo.wait_send()
    pltpu.make_async_copy(outbox, outbox, block_send).wait()
    pltpu.make_async_copy(patch_out, patch_out, patch_send).wait()


def correlate(freq, tables, jitter, early, jitter_out, surfaces_out, late, sem):
    pairs = early.shape[0]
    copies = [
        pltpu.make_async_copy(early, surfaces_out.at[pl.ds(0, pairs), 0, 0], sem.at[0]),
        pltpu.make_async_copy(jitter, jitter_out, sem.at[1]),
        pltpu.make_async_copy(late, surfaces_out.at[pairs, 0, 0], sem.at[2]),
    ]
    copies[0].start()
    copies[1].start()
    late[...] = surface(freq[0], freq[1], tables)
    copies[2].start()
    for copy in copies:
        copy.wait()


def per_device(section_pixels, jitter_index, drift_list, blend_weight, patch_col):
    _, row_count, row_width = section_pixels.shape
    sections = lax.axis_size("sec")
    tiles, rows_axis = lax.axis_size("tile"), lax.axis_size("row")
    owners = tiles * rows_axis
    moves = drift_list.shape[2]
    blocks = row_width // LANES
    chunks = len(row_chunks(row_count))
    pieces = len(load_pieces(row_count))
    sizes = (sections, tiles, rows_axis, row_count, row_width, moves)
    tables = dft_tables(PATCH)
    f32, bf16 = jnp.float32, jnp.bfloat16
    vmem = pl.BlockSpec(memory_space=pltpu.VMEM)
    anywhere = pl.BlockSpec(memory_space=pl.ANY)
    dma = pltpu.SemaphoreType.DMA
    between = pl.pallas_call(
        functools.partial(kernel, sizes),
        out_shape=(
            pltpu.VMEM((1, row_count), f32),
            pltpu.VMEM((2, 2 * PATCH, PATCH), f32),
            pltpu.VMEM((sections - 2, PATCH, PATCH), f32),
            pltpu.VMEM(tables.shape, bf16),
        ),
        in_specs=[anywhere] * 6,
        out_specs=(vmem,) * 4,
        scratch_shapes=[
            pltpu.VMEM((row_count, row_width), f32),
            pltpu.VMEM(jitter_index.shape, jnp.int32),
            pltpu.SMEM((1, 3, owners, moves), jnp.int32),
            pltpu.SMEM(blend_weight.shape, f32),
            pltpu.SMEM(patch_col.shape, jnp.int32),
            pltpu.VMEM((row_count, LANES), jnp.int32),
            pltpu.VMEM((blocks + 2, row_count + 8, LANES), f32),
            pltpu.VMEM((blocks, row_count + 8, LANES), f32),
            pltpu.VMEM((row_count, LANES), f32),
            pltpu.VMEM((row_count + 8, LANES), f32),
            pltpu.VMEM((row_count, LANES), f32),
            pltpu.VMEM((blocks, 8, LANES), f32),
            pltpu.VMEM((blocks, 1, LANES), f32),
            pltpu.VMEM((owners - 1, CAP, BLOCK, BLOCK), bf16),
            pltpu.VMEM((owners - 1, CAP, BLOCK, BLOCK), bf16),
            pltpu.VMEM((sections, owners * CAP + 1, 8, LANES), f32),
            pltpu.VMEM((sections, PATCH, LANES), f32),
            pltpu.VMEM((sections - 1, PATCH, PATCH), bf16),
            pltpu.VMEM((sections, PATCH, PATCH), bf16),
            pltpu.VMEM((sections - 2, 2 * PATCH, PATCH), f32),
            dma((pieces,)),
            dma,
            dma((4,)),
            dma((2,)),
            dma,
            dma((chunks,)),
            dma,
            dma((sections,)),
        ],
        compiler_params=pltpu.CompilerParams(collective_id=0, has_side_effects=True),
        name="section_patches",
    )(
        section_pixels,
        jitter_index,
        jnp.transpose(drift_list, (0, 3, 1, 2)),
        blend_weight,
        patch_col,
        tables,
    )
    jitter, freq, early, tables = [
        pltpu.with_memory_space_constraint(x, pltpu.VMEM) for x in between
    ]
    return pl.pallas_call(
        correlate,
        out_shape=(
            jax.ShapeDtypeStruct((1, row_count), f32),
            jax.ShapeDtypeStruct((sections - 1, 1, 1, PATCH, PATCH), f32),
        ),
        in_specs=[vmem] * 4,
        out_specs=(anywhere, anywhere),
        scratch_shapes=[pltpu.VMEM((PATCH, PATCH), f32), dma((3,))],
        name="section_correlation",
    )(freq, tables, jitter, early)


def solution(mesh):
    in_specs = (
        P(("groups", "sec"), ("tile", "row"), None),
        P(("groups", "sec"), ("tile", "row")),
        P(("groups", "sec"), None, None, None),
        P(("groups", "sec"), None, None),
        P(("tile", "row"), "groups"),
    )
    out_specs = (
        P(("groups", "sec"), ("tile", "row")),
        P("groups", ("tile", "row"), "sec", None, None),
    )
    return jax.shard_map(
        per_device, mesh=mesh, in_specs=in_specs, out_specs=out_specs, check_vma=False
    )
```

```python
import functools
import math

import jax
import jax.numpy as jnp
import numpy as np
from jax import lax
from jax.experimental import pallas as pl
from jax.experimental.pallas import tpu as pltpu
from jax.sharding import PartitionSpec as P

SEG = 512
PATCH = 128
BLOCK = 128
CAP = 2
LANES = 128
MESH = pl.DeviceIdType.MESH


def dft_tables(side):
    index = np.arange(side)
    angles = (index[:, None] * index[None, :] % side) * (2.0 * math.pi / side)
    cosine, sine = np.cos(angles), np.sin(angles)
    table = np.concatenate(
        [
            np.concatenate([cosine, sine], 1),
            np.concatenate([cosine, -sine], 1),
            np.concatenate([-sine, -cosine], 1),
        ],
        0,
    )
    high = table.astype(jnp.bfloat16)
    low = (table - high.astype(np.float64)).astype(jnp.bfloat16)
    return np.stack([high, low])


def dot(a, b):
    return jnp.dot(a, b, preferred_element_type=jnp.float32)


def split(a):
    high = a.astype(jnp.bfloat16)
    return high, (a - high.astype(jnp.float32)).astype(jnp.bfloat16)


def dot3(a, b):
    return dot(a[0], b[0]) + (dot(a[0], b[1]) + dot(a[1], b[0]))


def total(terms):
    terms = list(terms)
    while len(terms) > 1:
        terms = [
            terms[i] + terms[i + 1] if i + 1 < len(terms) else terms[i]
            for i in range(0, len(terms), 2)
        ]
    return terms[0]


def take(x, index):
    return jnp.take_along_axis(x, index, axis=1)


def row_chunks(row_count):
    cuts = [0, 16] + list(range(48, row_count - 16, 32)) + [row_count - 16, row_count]
    return [(a, b) for a, b in zip(cuts[:-1], cuts[1:])][::-1]


def load_pieces(row_count):
    cuts = [max(a - 8, 0) for a, _ in row_chunks(row_count)]
    return [(a, b) for a, b in zip(cuts[:-2] + [0], [row_count] + cuts[:-2])]


def forward(patch, tables):
    wide = tables[0, 0:PATCH, :], tables[1, 0:PATCH, :]
    square = tables[0, PATCH : 3 * PATCH, :], tables[1, PATCH : 3 * PATCH, :]
    first = dot(patch, wide[0]) + dot(patch, wide[1])
    stacked = jnp.concatenate([first[:, :PATCH], first[:, PATCH:]], 0)
    return dot3(square, split(stacked))


def surface(now, after, tables):
    wide = tables[0, 0:PATCH, :]
    square = tables[0, PATCH : 3 * PATCH, :]
    now_real, now_imag = now[0:PATCH], now[PATCH : 2 * PATCH]
    next_real, next_imag = after[0:PATCH], after[PATCH : 2 * PATCH]
    cross_real = now_real * next_real + now_imag * next_imag
    cross_imag = now_imag * next_real - now_real * next_imag
    magnitude = jnp.sqrt(cross_real * cross_real + cross_imag * cross_imag)
    mean = jnp.sum(jnp.sum(magnitude, axis=0, keepdims=True), axis=1, keepdims=True) * (
        1.0 / (PATCH * PATCH)
    )
    scaled = 1.0 / (magnitude + (0.5 * mean + 1e-06))
    damped = jnp.concatenate([cross_real * scaled, cross_imag * scaled], 1)
    back = dot(damped.astype(jnp.bfloat16), square)
    stacked = jnp.concatenate([back[:, :PATCH], back[:, PATCH:]], 0)
    return dot(wide, stacked.astype(jnp.bfloat16)) * (1.0 / PATCH)


def kernel(
    sizes,
    pixels,
    delays_hbm,
    drifts_hbm,
    weights_hbm,
    columns_hbm,
    tables_hbm,
    jitter_out,
    freq_out,
    early_out,
    tables,
    raw,
    delays,
    drifts,
    weights,
    columns,
    delay_rows,
    aligned,
    ahead,
    cross_sums,
    energies,
    jitter_rows,
    halo_out,
    halo_in,
    outbox,
    arrived,
    coefs,
    partial,
    patch_out,
    patch_in,
    freq,
    load_sem,
    table_sem,
    small_sem,
    halo_sem,
    block_send,
    block_recv,
    patch_send,
    patch_recv,
):
    sections, tiles, rows_axis, row_count, row_width, moves = sizes
    owners = tiles * rows_axis
    blocks = row_width // LANES
    per_seg = SEG // LANES
    segs = row_width // SEG
    slab_blocks = blocks // sections
    chunks = row_chunks(row_count)
    pieces = load_pieces(row_count)
    f32, bf16 = jnp.float32, jnp.bfloat16
    tile, row_at = lax.axis_index("tile"), lax.axis_index("row")
    me = tile * rows_axis + row_at
    section = lax.axis_index("sec")

    def band_device(band):
        return {"tile": band // rows_axis, "row": band % rows_axis}

    band_steps = [(t, r) for t in range(tiles) for r in range(rows_axis)][1:]
    band_steps.sort(key=lambda step: -min(step[0], tiles - step[0]))

    def slot_of(step):
        return step[0] * rows_axis + step[1] - 1

    def band_at(step):
        return (tile + step[0]) % tiles * rows_axis + (row_at + step[1]) % rows_axis

    def band_from(step):
        return (tile - step[0] + tiles) % tiles * rows_axis + (
            row_at - step[1] + rows_axis
        ) % rows_axis

    upper = 2 * section // sections
    targets = []
    for i in range(sections - 1):
        up = i + (i + sections - section) // sections
        down = sections - 1 - i
        down = down - 1 + (down + sections - section - 1) // sections
        targets.append(upper * up + (1 - upper) * down)
    targets.append(section)

    table_copy = pltpu.make_async_copy(tables_hbm, tables, table_sem)
    loads = [
        pltpu.make_async_copy(
            pixels.at[0, pl.ds(a, b - a)], raw.at[pl.ds(a, b - a)], load_sem.at[i]
        )
        for i, (a, b) in enumerate(pieces)
    ]
    small_copies = [
        pltpu.make_async_copy(source, target, small_sem.at[i])
        for i, (source, target) in enumerate(
            (
                (delays_hbm, delays),
                (drifts_hbm, drifts),
                (weights_hbm, weights),
                (columns_hbm, columns),
            )
        )
    ]
    small_copies[0].start()
    loads[0].start()
    for copy in small_copies[1:]:
        copy.start()
    for copy in loads[1:]:
        copy.start()
    table_copy.start()

    barrier = pltpu.get_barrier_semaphore()
    for step in range(1, owners):
        pl.semaphore_signal(
            barrier, inc=1, device_id=band_device((me + step) % owners), device_id_type=MESH
        )
    for step in range(1, sections):
        pl.semaphore_signal(
            barrier, inc=1, device_id={"sec": (section + step) % sections}, device_id_type=MESH
        )

    lane = lax.broadcasted_iota(jnp.int32, (8, LANES), 1)
    first_lane, last_lane = lane == 0, lane == LANES - 1
    to_right, to_left = (lane + 1) & (LANES - 1), (lane + LANES - 1) & (LANES - 1)
    zero = jnp.zeros((8, LANES), f32)
    for g in range(0, row_count + 8, 8):
        aligned[0, g : g + 8, :] = zero
        aligned[blocks + 1, g : g + 8, :] = zero
    small_copies[0].wait()
    delay_rows[...] = (
        jnp.broadcast_to(delays[...].astype(f32), (LANES, row_count)).T
    ).astype(jnp.int32)

    def shifted(g):
        start = g * 8
        delay = delay_rows[start : start + 8, :]
        values = [raw[start : start + 8, v * LANES : (v + 1) * LANES] for v in range(blocks)]
        near = lane + delay
        here = [take(x, near & (LANES - 1)) for x in values] + [zero]
        far = near + 1
        there = [take(x, far & (LANES - 1)) for x in values] + [zero]
        near_kept, far_kept = near < LANES, far < LANES
        now, after = [], []
        for v in range(blocks):
            now.append(jnp.where(near_kept, here[v], here[v + 1]))
            x = jnp.where(far_kept, there[v], there[v + 1])
            if v % per_seg == per_seg - 1:
                x = jnp.where(last_lane, there[v + 1 - per_seg], x)
            after.append(x)
        return now, after

    def keep(g, now, after):
        rows = slice(g * 8 + 8, g * 8 + 16)
        for v in range(blocks):
            aligned[v + 1, rows, :] = now[v]
            ahead[v, rows, :] = after[v]
        energies[rows, :] = total(x * x for x in now)

    def compare(g, now=None, after=None):
        start = g * 8
        terms = []
        for v in range(blocks):
            x = now[v] if now else aligned[v + 1, start + 8 : start + 16, :]
            x_after = after[v] if after else ahead[v, start + 8 : start + 16, :]
            above = aligned[v + 1, start + 7 : start + 15, :]
            above_after = ahead[v, start + 7 : start + 15, :]
            terms.append(above * x_after - above_after * x)
        cross_sums[start : start + 8, :] = total(terms)

    halo = pltpu.make_async_remote_copy(
        src_ref=halo_out.at[:, pl.ds(7, 1)],
        dst_ref=halo_in,
        send_sem=halo_sem.at[0],
        recv_sem=halo_sem.at[1],
        device_id=band_device((me + 1) % owners),
        device_id_type=MESH,
    )

    def pick(hits, values, default):
        first = second = default
        for hit, value in zip(hits[::-1], values[::-1]):
            second = jnp.where(hit, first, second)
            first = jnp.where(hit, value, first)
        return first, second

    sources = {}

    def find_sources():
        own_sources = [drifts[0, 0, me, k] for k in range(moves)]
        own_owners = [drifts[0, 1, me, k] for k in range(moves)]
        found = {}
        for step in band_steps + [(0, 0)]:
            owner = band_at(step)
            picked = pick([o == owner for o in own_owners], own_sources, jnp.int32(0))
            for rank in range(CAP):
                found[step, rank] = picked[rank]
        return found

    def corrected(block, start):
        rows = slice(start + 8, start + 16)
        before, x, after = [aligned[block + i, rows, :] for i in range(3)]
        left = take(jnp.where(last_lane, before, x), to_left)
        right = take(jnp.where(first_lane, after, x), to_right)
        return x - jitter_rows[start : start + 8, :] * (right - left)

    def finish(a, b):
        numerator = jnp.sum(cross_sums[a:b, :], axis=1, keepdims=True) * (-0.5 / segs)
        power = energies[a + 8 : b + 8, :] + energies[a + 7 : b + 7, :]
        power = jnp.sum(power, axis=1, keepdims=True) * (0.5 / segs)
        jitter = jnp.broadcast_to(numerator / (power + 1e-05), (b - a, LANES))
        jitter_rows[a:b, :] = 0.5 * jitter

    def fill_blocks(c):
        a, b = chunks[c]
        for step in band_steps:
            for rank in range(CAP):
                for start in range(a, b, 16):
                    pair = [corrected(sources[step, rank], start + i) for i in (0, 8)]
                    outbox[slot_of(step), rank, start : start + 16, :] = jnp.concatenate(
                        pair, 0
                    ).astype(bf16)

    def send_blocks(c):
        a, b = chunks[c]
        for step in band_steps:
            slot = slot_of(step)
            copy = pltpu.make_async_remote_copy(
                src_ref=outbox.at[slot, :, pl.ds(a, b - a)],
                dst_ref=arrived.at[slot, :, pl.ds(a, b - a)],
                send_sem=block_send,
                recv_sem=block_recv.at[c],
                device_id=band_device(band_at(step)),
                device_id_type=MESH,
            )
            copy.start()

    steps = [(0, 0)] + band_steps
    keys = [(step, rank) for step in steps for rank in range(CAP)]

    blocks_at, starts = [], []

    def weigh():
        for target in targets:
            offset = columns[0, target]
            blocks_at.append(target * slab_blocks + offset // LANES)
            starts.append(offset % LANES)
        found = {}
        for step in steps:
            band = band_from(step)
            hits = [drifts[0, 1, band, k] == me for k in range(moves)]
            picked = pick(hits, [drifts[0, 2, band, k] for k in range(moves)], jnp.int32(-1))
            heavy = pick(hits, [weights[0, band, k] for k in range(moves)], jnp.float32(0.0))
            for rank in range(CAP):
                found[step, rank] = picked[rank], heavy[rank]
        for p in range(sections):
            under = jnp.where(lane >= starts[p], blocks_at[p], blocks_at[p] + 1)
            shares = [jnp.where(under == found[key][0], found[key][1], 0.0) for key in keys]
            scale = 1.0 / (1.0 + total(shares))
            coefs[p, len(keys)] = scale
            for i, share in enumerate(shares):
                coefs[p, i] = share * scale

    def own_part(a, b):
        for start in range(a, b, 8):
            rows = slice(start + 8, start + 16)
            half = jitter_rows[start : start + 8, :]
            mine = [
                corrected(sources[(0, 0), rank], start).astype(bf16).astype(f32)
                for rank in range(CAP)
            ]
            for p in range(sections):
                block, offset = blocks_at[p], starts[p]
                before, x, after = [aligned[block + i, rows, :] for i in range(3)]
                left = jnp.where(lane >= offset - 1, x, after)
                left = jnp.where((lane - offset) == LANES - 1, before, left)
                left = take(left, to_left)
                right = take(jnp.where(lane > offset, x, after), to_right)
                value = jnp.where(lane >= offset, x, after) - half * (right - left)
                value = value.astype(bf16).astype(f32) * coefs[p, len(keys)]
                for rank in range(CAP):
                    value = value + coefs[p, rank] * mine[rank]
                partial[p, start : start + 8, :] = value

    def send_patches(c):
        a, b = chunks[c]
        pltpu.make_async_copy(
            arrived.at[:, :, pl.ds(a, b - a)], arrived.at[:, :, pl.ds(a, b - a)], block_recv.at[c]
        ).wait()
        for start in range(a, b, 16):
            blocks_in = [
                arrived[slot_of(step), rank, start : start + 16, :].astype(f32)
                for step, rank in keys[CAP:]
            ]
            for p in range(sections):
                turn = (lane + starts[p]) & (LANES - 1)
                shares = [coefs[p, CAP + i] for i in range(len(blocks_in))]
                values = []
                for i in (0, 8):
                    terms = [share * x[i : i + 8] for share, x in zip(shares, blocks_in)]
                    values.append(take(partial[p, start + i : start + i + 8, :] + total(terms), turn))
                patch = jnp.concatenate(values, 0).astype(bf16)
                if p < sections - 1:
                    patch_out[p, start : start + 16, :] = patch
                else:
                    patch_in[section, start : start + 16, :] = patch
        for p, target in enumerate(targets[:-1]):
            pltpu.make_async_remote_copy(
                src_ref=patch_out.at[p, pl.ds(a, b - a)],
                dst_ref=patch_in.at[section, pl.ds(a, b - a)],
                send_sem=patch_send,
                recv_sem=patch_recv.at[section],
                device_id={"sec": target},
                device_id_type=MESH,
            ).start()

    aligned_groups = set()

    def group(g):
        now, after = shifted(g)
        keep(g, now, after)
        aligned_groups.add(g)
        return now, after

    def above(c):
        group(chunks[c][0] // 8 - 1)

    def groups(c, part=None):
        a, b = chunks[c][0] // 8, chunks[c][1] // 8
        todo = list(range(a, b))
        if part is not None:
            half = (b - a) // 2 - 1
            todo = todo[:half] if part == 0 else todo[half:]
        for g in todo:
            if g in aligned_groups:
                compare(g)
            else:
                compare(g, *group(g))

    def finish_and_fill(c):
        finish(*chunks[c])
        fill_blocks(c)

    def halo_rows():
        shown = jnp.where(me == 0, 0.0, 1.0)
        rows = [shown * jnp.broadcast_to(halo_in[v], (8, LANES)) for v in range(blocks)]
        turned = [take(x, to_right) for x in rows]
        for v in range(blocks):
            follows = v + 1 - per_seg if v % per_seg == per_seg - 1 else v + 1
            aligned[v + 1, 0:8, :] = rows[v]
            ahead[v, 0:8, :] = jnp.where(last_lane, turned[follows], turned[v])
        energies[0:8, :] = total(x * x for x in rows)

    last = len(chunks) - 1
    loads[0].wait()
    for copy in small_copies[1:]:
        copy.wait()
    sources.update(find_sources())
    above(0)
    groups(0)
    for v in range(blocks):
        halo_out[v, :, :] = aligned[v + 1, row_count : row_count + 8, :]
    finish_and_fill(0)
    pl.semaphore_wait(barrier, owners + sections - 2)
    send_blocks(0)
    halo.start()
    for load in loads[1:]:
        load.wait()
    weigh()
    above(1)
    groups(1)
    for c in range(1, last):
        finish_and_fill(c)
        if c < last - 1:
            above(c + 1)
            groups(c + 1, 0)
        else:
            group(0)
            own_part(*chunks[0])
        send_blocks(c)
        if c < last - 1:
            groups(c + 1, 1)
    halo.wait_recv()
    halo_rows()
    groups(last)
    finish_and_fill(last)
    send_blocks(last)
    for c in range(1, last + 1):
        own_part(*chunks[c])
    for c in range(last + 1):
        send_patches(c)

    jitter_out[...] = 2.0 * jitter_rows[...].T[0:1, :]
    table_copy.wait()
    for s in range(sections):

        @pl.when(section != s)
        def _():
            pltpu.make_async_copy(patch_in.at[s], patch_in.at[s], patch_recv.at[s]).wait()

        if s > 1:
            early_out[s - 2] = surface(freq[s - 2], freq[s - 1], tables)
        spectrum = forward(patch_in[s], tables)
        freq[s] = spectrum
        if s > sections - 3:
            freq_out[s - sections + 2] = spectrum

    halo.wait_send()
    pltpu.make_async_copy(outbox, outbox, block_send).wait()
    pltpu.make_async_copy(patch_out, patch_out, patch_send).wait()


def correlate(freq, tables, jitter, early, jitter_out, surfaces_out, late, sem):
    pairs = early.shape[0]
    copies = [
        pltpu.make_async_copy(early, surfaces_out.at[pl.ds(0, pairs), 0, 0], sem.at[0]),
        pltpu.make_async_copy(jitter, jitter_out, sem.at[1]),
        pltpu.make_async_copy(late, surfaces_out.at[pairs, 0, 0], sem.at[2]),
    ]
    copies[0].start()
    copies[1].start()
    late[...] = surface(freq[0], freq[1], tables)
    copies[2].start()
    for copy in copies:
        copy.wait()


def per_device(section_pixels, jitter_index, drift_list, blend_weight, patch_col):
    _, row_count, row_width = section_pixels.shape
    sections = lax.axis_size("sec")
    tiles, rows_axis = lax.axis_size("tile"), lax.axis_size("row")
    owners = tiles * rows_axis
    moves = drift_list.shape[2]
    blocks = row_width // LANES
    chunks = len(row_chunks(row_count))
    pieces = len(load_pieces(row_count))
    sizes = (sections, tiles, rows_axis, row_count, row_width, moves)
    tables = dft_tables(PATCH)
    f32, bf16 = jnp.float32, jnp.bfloat16
    vmem = pl.BlockSpec(memory_space=pltpu.VMEM)
    anywhere = pl.BlockSpec(memory_space=pl.ANY)
    dma = pltpu.SemaphoreType.DMA
    between = pl.pallas_call(
        functools.partial(kernel, sizes),
        out_shape=(
            pltpu.VMEM((1, row_count), f32),
            pltpu.VMEM((2, 2 * PATCH, PATCH), f32),
            pltpu.VMEM((sections - 2, PATCH, PATCH), f32),
            pltpu.VMEM(tables.shape, bf16),
        ),
        in_specs=[anywhere] * 6,
        out_specs=(vmem,) * 4,
        scratch_shapes=[
            pltpu.VMEM((row_count, row_width), f32),
            pltpu.VMEM(jitter_index.shape, jnp.int32),
            pltpu.SMEM((1, 3, owners, moves), jnp.int32),
            pltpu.SMEM(blend_weight.shape, f32),
            pltpu.SMEM(patch_col.shape, jnp.int32),
            pltpu.VMEM((row_count, LANES), jnp.int32),
            pltpu.VMEM((blocks + 2, row_count + 8, LANES), f32),
            pltpu.VMEM((blocks, row_count + 8, LANES), f32),
            pltpu.VMEM((row_count, LANES), f32),
            pltpu.VMEM((row_count + 8, LANES), f32),
            pltpu.VMEM((row_count, LANES), f32),
            pltpu.VMEM((blocks, 8, LANES), f32),
            pltpu.VMEM((blocks, 1, LANES), f32),
            pltpu.VMEM((owners - 1, CAP, BLOCK, BLOCK), bf16),
            pltpu.VMEM((owners - 1, CAP, BLOCK, BLOCK), bf16),
            pltpu.VMEM((sections, owners * CAP + 1, 8, LANES), f32),
            pltpu.VMEM((sections, PATCH, LANES), f32),
            pltpu.VMEM((sections - 1, PATCH, PATCH), bf16),
            pltpu.VMEM((sections, PATCH, PATCH), bf16),
            pltpu.VMEM((sections, 2 * PATCH, PATCH), f32),
            dma((pieces,)),
            dma,
            dma((4,)),
            dma((2,)),
            dma,
            dma((chunks,)),
            dma,
            dma((sections,)),
        ],
        compiler_params=pltpu.CompilerParams(collective_id=0, has_side_effects=True),
        name="section_patches",
    )(
        section_pixels,
        jitter_index,
        jnp.transpose(drift_list, (0, 3, 1, 2)),
        blend_weight,
        patch_col,
        tables,
    )
    jitter, freq, early, tables = [
        pltpu.with_memory_space_constraint(x, pltpu.VMEM) for x in between
    ]
    return pl.pallas_call(
        correlate,
        out_shape=(
            jax.ShapeDtypeStruct((1, row_count), f32),
            jax.ShapeDtypeStruct((sections - 1, 1, 1, PATCH, PATCH), f32),
        ),
        in_specs=[vmem] * 4,
        out_specs=(anywhere, anywhere),
        scratch_shapes=[pltpu.VMEM((PATCH, PATCH), f32), dma((3,))],
        name="section_correlation",
    )(freq, tables, jitter, early)


def solution(mesh):
    in_specs = (
        P(("groups", "sec"), ("tile", "row"), None),
        P(("groups", "sec"), ("tile", "row")),
        P(("groups", "sec"), None, None, None),
        P(("groups", "sec"), None, None),
        P(("tile", "row"), "groups"),
    )
    out_specs = (
        P(("groups", "sec"), ("tile", "row")),
        P("groups", ("tile", "row"), "sec", None, None),
    )
    return jax.shard_map(
        per_device, mesh=mesh, in_specs=in_specs, out_specs=out_specs, check_vma=False
    )
```

```python
import functools
import math

import jax
import jax.numpy as jnp
import numpy as np
from jax import lax
from jax.experimental import pallas as pl
from jax.experimental.pallas import tpu as pltpu
from jax.sharding import PartitionSpec as P

SEG = 512
PATCH = 128
BLOCK = 128
CAP = 2
LANES = 128
MESH = pl.DeviceIdType.MESH


def dft_tables(side):
    index = np.arange(side)
    angles = (index[:, None] * index[None, :] % side) * (2.0 * math.pi / side)
    cosine, sine = np.cos(angles), np.sin(angles)
    table = np.concatenate(
        [
            np.concatenate([cosine, sine], 1),
            np.concatenate([cosine, -sine], 1),
            np.concatenate([-sine, -cosine], 1),
        ],
        0,
    )
    high = table.astype(jnp.bfloat16)
    low = (table - high.astype(np.float64)).astype(jnp.bfloat16)
    return np.stack([high, low])


def dot(a, b):
    return jnp.dot(a, b, preferred_element_type=jnp.float32)


def split(a):
    high = a.astype(jnp.bfloat16)
    return high, (a - high.astype(jnp.float32)).astype(jnp.bfloat16)


def dot3(a, b):
    return dot(a[0], b[0]) + (dot(a[0], b[1]) + dot(a[1], b[0]))


def total(terms):
    terms = list(terms)
    while len(terms) > 1:
        terms = [
            terms[i] + terms[i + 1] if i + 1 < len(terms) else terms[i]
            for i in range(0, len(terms), 2)
        ]
    return terms[0]


def take(x, index):
    return jnp.take_along_axis(x, index, axis=1)


def row_chunks(row_count):
    cuts = [0, 16] + list(range(48, row_count - 16, 32)) + [row_count - 16, row_count]
    return [(a, b) for a, b in zip(cuts[:-1], cuts[1:])][::-1]


def load_pieces(row_count):
    cuts = [row_count] + list(range(row_count - 24, 0, -32))
    return [(a, b) for a, b in zip(cuts[1:-1] + [0], cuts[:-1])]


def downward(section, sections):
    return (section + sections - 1) // sections


def forward(patch, tables):
    wide = tables[0, 0:PATCH, :], tables[1, 0:PATCH, :]
    square = tables[0, PATCH : 3 * PATCH, :], tables[1, PATCH : 3 * PATCH, :]
    first = dot(patch, wide[0]) + dot(patch, wide[1])
    stacked = jnp.concatenate([first[:, :PATCH], first[:, PATCH:]], 0)
    return dot3(square, split(stacked))


def surface(now, after, tables):
    wide = tables[0, 0:PATCH, :]
    square = tables[0, PATCH : 3 * PATCH, :]
    now_real, now_imag = now[0:PATCH], now[PATCH : 2 * PATCH]
    next_real, next_imag = after[0:PATCH], after[PATCH : 2 * PATCH]
    cross_real = now_real * next_real + now_imag * next_imag
    cross_imag = now_imag * next_real - now_real * next_imag
    magnitude = jnp.sqrt(cross_real * cross_real + cross_imag * cross_imag)
    mean = jnp.sum(jnp.sum(magnitude, axis=0, keepdims=True), axis=1, keepdims=True) * (
        1.0 / (PATCH * PATCH)
    )
    scaled = 1.0 / (magnitude + (0.5 * mean + 1e-06))
    damped = jnp.concatenate([cross_real * scaled, cross_imag * scaled], 1)
    back = dot(damped.astype(jnp.bfloat16), square)
    stacked = jnp.concatenate([back[:, :PATCH], back[:, PATCH:]], 0)
    return dot(wide, stacked.astype(jnp.bfloat16)) * (1.0 / PATCH)


def kernel(
    sizes,
    pixels,
    delays_hbm,
    drifts_hbm,
    weights_hbm,
    columns_hbm,
    tables_hbm,
    jitter_out,
    freq_out,
    early_out,
    tables,
    raw,
    delays,
    drifts,
    weights,
    columns,
    delay_rows,
    aligned,
    ahead,
    cross_sums,
    energies,
    jitter_rows,
    halo_out,
    halo_in,
    outbox,
    arrived,
    spots_out,
    spots_in,
    base_out,
    base_in,
    coefs,
    patch_out,
    patch_in,
    freq,
    load_sem,
    table_sem,
    small_sem,
    halo_sem,
    block_send,
    block_recv,
    side_send,
    side_recv,
    patch_send,
    patch_recv,
):
    sections, tiles, rows_axis, row_count, row_width, moves = sizes
    owners = tiles * rows_axis
    blocks = row_width // LANES
    per_seg = SEG // LANES
    segs = row_width // SEG
    slab_blocks = blocks // sections
    chunks = row_chunks(row_count)
    pieces = load_pieces(row_count)
    f32, bf16 = jnp.float32, jnp.bfloat16
    tile, row_at = lax.axis_index("tile"), lax.axis_index("row")
    me = tile * rows_axis + row_at
    section = lax.axis_index("sec")

    def band_device(band):
        return {"tile": band // rows_axis, "row": band % rows_axis}

    blends = row_at == rows_axis - 1
    others = [i + (i + owners - me) // owners for i in range(owners - 1)]

    def tile_at(step):
        return (tile + step) % tiles

    def blender(at):
        return {"tile": at, "row": rows_axis - 1}

    def place_at(at):
        return me - (me - (at + 1) * rows_axis + owners) // owners

    table_copy = pltpu.make_async_copy(tables_hbm, tables, table_sem)
    loads = [
        pltpu.make_async_copy(
            pixels.at[0, pl.ds(a, b - a)], raw.at[pl.ds(a, b - a)], load_sem.at[i]
        )
        for i, (a, b) in enumerate(pieces)
    ]
    small_copies = [
        pltpu.make_async_copy(source, target, small_sem.at[i])
        for i, (source, target) in enumerate(
            (
                (delays_hbm, delays),
                (drifts_hbm, drifts),
                (weights_hbm, weights),
                (columns_hbm, columns),
            )
        )
    ]
    small_copies[0].start()
    loads[0].start()
    barrier = pltpu.get_barrier_semaphore()
    for step in range(1, sections):
        far = (section + step) % sections
        pl.semaphore_signal(
            barrier, inc=1, device_id={"sec": far, "row": rows_axis - 1}, device_id_type=MESH
        )
    for copy in small_copies[1:] + loads[1:2]:
        copy.start()
    for band in others:
        pl.semaphore_signal(barrier, inc=1, device_id=band_device(band), device_id_type=MESH)

    @pl.when(blends)
    def _():
        for step in range(1, sections):
            for r in range(rows_axis - 1):
                far = {"sec": (section + step) % sections, "row": r}
                pl.semaphore_signal(barrier, inc=1, device_id=far, device_id_type=MESH)

    for copy in loads[2:]:
        copy.start()
    table_copy.start()

    lane = lax.broadcasted_iota(jnp.int32, (8, LANES), 1)
    first_lane, last_lane = lane == 0, lane == LANES - 1
    to_right, to_left = (lane + 1) & (LANES - 1), (lane + LANES - 1) & (LANES - 1)
    zero = jnp.zeros((8, LANES), f32)
    for g in range(0, row_count + 8, 8):
        aligned[0, g : g + 8, :] = zero
        aligned[blocks + 1, g : g + 8, :] = zero
    small_copies[0].wait()
    delay_rows[...] = (
        jnp.broadcast_to(delays[...].astype(f32), (LANES, row_count)).T
    ).astype(jnp.int32)

    def shifted(g):
        start = g * 8
        delay = delay_rows[start : start + 8, :]
        values = [raw[start : start + 8, v * LANES : (v + 1) * LANES] for v in range(blocks)]
        near = lane + delay
        here = [take(x, near & (LANES - 1)) for x in values] + [zero]
        far = near + 1
        there = [take(x, far & (LANES - 1)) for x in values] + [zero]
        near_kept, far_kept = near < LANES, far < LANES
        now, after = [], []
        for v in range(blocks):
            now.append(jnp.where(near_kept, here[v], here[v + 1]))
            x = jnp.where(far_kept, there[v], there[v + 1])
            if v % per_seg == per_seg - 1:
                x = jnp.where(last_lane, there[v + 1 - per_seg], x)
            after.append(x)
        return now, after

    def keep(g, now, after):
        rows = slice(g * 8 + 8, g * 8 + 16)
        for v in range(blocks):
            aligned[v + 1, rows, :] = now[v]
            ahead[v, rows, :] = after[v]
        energies[rows, :] = total(x * x for x in now)

    def compare(g, now=None, after=None):
        start = g * 8
        terms = []
        for v in range(blocks):
            x = now[v] if now else aligned[v + 1, start + 8 : start + 16, :]
            x_after = after[v] if after else ahead[v, start + 8 : start + 16, :]
            above = aligned[v + 1, start + 7 : start + 15, :]
            above_after = ahead[v, start + 7 : start + 15, :]
            terms.append(above * x_after - above_after * x)
        cross_sums[start : start + 8, :] = total(terms)

    halo = pltpu.make_async_remote_copy(
        src_ref=halo_out.at[:, pl.ds(7, 1)],
        dst_ref=halo_in,
        send_sem=halo_sem.at[0],
        recv_sem=halo_sem.at[1],
        device_id=band_device((me + 1) % owners),
        device_id_type=MESH,
    )

    def pick(hits, values, default):
        first = second = default
        for hit, value in zip(hits[::-1], values[::-1]):
            second = jnp.where(hit, first, second)
            first = jnp.where(hit, value, first)
        return first, second

    sources = {}

    def find_sources():
        own_sources = [drifts[0, 0, me, k] for k in range(moves)]
        own_owners = [drifts[0, 1, me, k] for k in range(moves)]
        for step in range(tiles):
            for r in range(rows_axis):
                band = tile_at(step) * rows_axis + r
                picked = pick([o == band for o in own_owners], own_sources, jnp.int32(0))
                for rank in range(CAP):
                    sources[step, r, rank] = picked[rank]

    def corrected(block, start):
        rows = slice(start + 8, start + 16)
        before, x, after = [aligned[block + i, rows, :] for i in range(3)]
        left = take(jnp.where(last_lane, before, x), to_left)
        right = take(jnp.where(first_lane, after, x), to_right)
        return x - jitter_rows[start : start + 8, :] * (right - left)

    def finish(a, b):
        numerator = jnp.sum(cross_sums[a:b, :], axis=1, keepdims=True) * (-0.5 / segs)
        power = energies[a + 8 : b + 8, :] + energies[a + 7 : b + 7, :]
        power = jnp.sum(power, axis=1, keepdims=True) * (0.5 / segs)
        jitter = jnp.broadcast_to(numerator / (power + 1e-05), (b - a, LANES))
        jitter_rows[a:b, :] = 0.5 * jitter

    def fill_blocks(step, r, c):
        a, b = chunks[c]
        for rank in range(CAP):
            for start in range(a, b, 16):
                block = sources[step, r, rank]
                pair = [corrected(block, start + half) for half in (0, 8)]
                outbox[step, r, rank, start : start + 16, :] = jnp.concatenate(pair, 0).astype(bf16)

    def send_blocks(step, sent):
        at = tile_at(step)

        def start():
            for r, c in sent:
                a, b = chunks[c]
                pltpu.make_async_remote_copy(
                    src_ref=outbox.at[step, r, :, pl.ds(a, b - a)],
                    dst_ref=arrived.at[r, place_at(at), :, pl.ds(a, b - a)],
                    send_sem=block_send,
                    recv_sem=block_recv.at[r, c],
                    device_id=blender(at),
                    device_id_type=MESH,
                ).start()

        if step:
            start()
        else:
            pl.when(row_at != rows_axis - 1)(start)

    def fill_base(patches):
        for p in patches:
            offset = columns[0, p] % LANES
            block = p * slab_blocks + columns[0, p] // LANES
            for start in range(0, row_count, 16):
                pair = []
                for at in (start, start + 8):
                    rows = slice(at + 8, at + 16)
                    before, x, after = [aligned[block + i, rows, :] for i in range(3)]
                    left = jnp.where(lane >= offset - 1, x, after)
                    left = jnp.where((lane - offset) == LANES - 1, before, left)
                    left = take(left, to_left)
                    right = take(jnp.where(lane > offset, x, after), to_right)
                    half = jitter_rows[at : at + 8, :]
                    pair.append(jnp.where(lane >= offset, x, after) - half * (right - left))
                base_out[p, start : start + 16, :] = jnp.concatenate(pair, 0).astype(bf16)

    def side_copy(source, target, i):
        return pltpu.make_async_remote_copy(
            src_ref=source,
            dst_ref=target,
            send_sem=side_send.at[i],
            recv_sem=side_recv.at[i],
            device_id=blender(tile),
            device_id_type=MESH,
        )

    row_slot = row_at % max(rows_axis - 1, 1)
    spots_copy = side_copy(spots_out, spots_in.at[row_slot], 0)
    base_copies = [
        side_copy(base_out.at[pl.ds(0, 1)], base_in.at[row_slot, pl.ds(0, 1)], 1),
        side_copy(
            base_out.at[pl.ds(1, sections - 1)], base_in.at[row_slot, pl.ds(1, sections - 1)], 2
        ),
    ]

    keys = [(i, rank) for i in range(owners) for rank in range(CAP)]

    def spot(r, p):
        spots = spots_out if r == rows_axis - 1 else spots_in.at[r]
        column = jnp.broadcast_to(spots[p : p + 1, :], (8, LANES)).astype(jnp.int32)
        return column & (LANES - 1), p * slab_blocks + column // LANES

    def weigh(r):
        found = {}
        owner = tile * rows_axis + r
        for i, band in enumerate([me] + others):
            hits = [drifts[0, 1, band, k] == owner for k in range(moves)]
            picked = pick(hits, [drifts[0, 2, band, k] for k in range(moves)], jnp.int32(-1))
            heavy = pick(hits, [weights[0, band, k] for k in range(moves)], jnp.float32(0.0))
            for rank in range(CAP):
                found[i, rank] = picked[rank], heavy[rank]
        for p in range(sections):
            first, block = spot(r, p)
            under = jnp.where(lane >= first, block, block + 1)
            shares = [jnp.where(under == found[key][0], found[key][1], 0.0) for key in keys]
            scale = 1.0 / (1.0 + total(shares))
            coefs[r, p, len(keys)] = scale
            for i, share in enumerate(shares):
                coefs[r, p, i] = share * scale

    def wait_blocks(r, c):
        a, b = chunks[c]
        landed = arrived.at[r, :, :, pl.ds(a, b - a)]
        pltpu.make_async_copy(landed, landed, block_recv.at[r, c]).wait()

    def blend(r, patches, a, b):
        turns = [(lane + spot(r, p)[0]) & (LANES - 1) for p in patches]
        for start in range(a, b, 16):
            rows = slice(start, start + 16)
            moved = [outbox[0, r, rank, rows, :].astype(f32) for rank in range(CAP)]
            moved += [arrived[r, i - 1, rank, rows, :].astype(f32) for i, rank in keys[CAP:]]
            for p, turn in zip(patches, turns):
                base = base_out[p, rows, :] if r == rows_axis - 1 else base_in[r, p, rows, :]
                shares = [coefs[r, p, i] for i in range(len(keys) + 1)]
                values = []
                for i in (0, 8):
                    terms = [share * x[i : i + 8] for share, x in zip(shares, moved)]
                    terms.append(shares[-1] * base[i : i + 8].astype(f32))
                    values.append(take(total(terms), turn))
                patch_out[r * sections + p, rows, :] = jnp.concatenate(values, 0).astype(bf16)

    def send_patch(r, p, a, b):
        @pl.when((section != p) | (r != rows_axis - 1))
        def _():
            pltpu.make_async_remote_copy(
                src_ref=patch_out.at[r * sections + p, pl.ds(a, b - a)],
                dst_ref=patch_in.at[section, pl.ds(a, b - a)],
                send_sem=patch_send,
                recv_sem=patch_recv.at[section],
                device_id={"sec": p, "row": r},
                device_id_type=MESH,
            ).start()

    aligned_groups = set()

    def group(g):
        now, after = shifted(g)
        keep(g, now, after)
        aligned_groups.add(g)
        return now, after

    loaded = 0

    def need(row):
        nonlocal loaded
        while not loaded or pieces[loaded - 1][0] > row:
            loads[loaded].wait()
            loaded += 1

    def groups(c):
        a, b = chunks[c][0] // 8, chunks[c][1] // 8
        for g in range(b - 1, max(a, 1) - 2, -1):
            if g not in aligned_groups:
                need(g * 8)
                group(g)
        for g in range(a, b):
            compare(g)

    def halo_rows():
        rows = [jnp.broadcast_to(halo_in[v], (8, LANES)) for v in range(blocks)]
        turned = [take(x, to_right) for x in rows]
        for v in range(blocks):
            follows = v + 1 - per_seg if v % per_seg == per_seg - 1 else v + 1
            aligned[v + 1, 0:8, :] = rows[v]
            ahead[v, 0:8, :] = jnp.where(last_lane, turned[follows], turned[v])
        energies[0:8, :] = total(x * x for x in rows)

    last = len(chunks) - 1
    groups(0)
    for v in range(blocks):
        halo_out[v, :, :] = aligned[v + 1, row_count : row_count + 8, :]
    for copy in small_copies[1:]:
        copy.wait()
    find_sources()
    for p in range(sections):
        spots_out[p : p + 1, :] = jnp.full((1, LANES), columns[0, p]).astype(f32)
    entered = (owners - 1) + (sections - 1) * (1 + (rows_axis - 1) * (row_at // (rows_axis - 1)))
    pl.semaphore_wait(barrier, entered)

    @pl.when(me < owners - 1)
    def _():
        halo.start()

    @pl.when(row_at != rows_axis - 1)
    def _():
        spots_copy.start()

    early = range(last - 2)
    rest = [(r, c) for r in range(1, rows_axis) for c in range(last + 1) if c not in early]
    for c in range(last):
        now = [(r, c) for r in range(rows_axis if c in early else 1)]
        finish(*chunks[c])
        for r, c in now:
            fill_blocks(1, r, c)
        if c == 0:
            send_blocks(1, now)
        if c + 1 < last:
            groups(c + 1)
        else:
            group(0)
        if c:
            send_blocks(1, now)

    @pl.when(me > 0)
    def _():
        halo.wait_recv()

    @pl.when(me == 0)
    def _():
        halo_in[...] = jnp.zeros((blocks, 1, LANES), f32)

    halo_rows()
    for g in range(chunks[last][1] // 8):
        compare(g)
    finish(*chunks[last])
    fill_blocks(1, 0, last)
    send_blocks(1, [(0, last)])
    fill_base([0])

    @pl.when(row_at != rows_axis - 1)
    def _():
        base_copies[0].start()

    def send_all(step, sent):
        for r, c in sent:
            fill_blocks(step, r, c)
        send_blocks(step, sent)

    send_all(0, [(0, c) for c in range(last + 1)])
    send_all(1, rest)
    send_all(0, [(r, c) for r in range(1, rows_axis) for c in range(last + 1)])
    for step in range(2, tiles):
        send_all(step, [(r, c) for r in range(rows_axis) for c in range(last + 1)])
    fill_base(range(1, sections))

    @pl.when(row_at != rows_axis - 1)
    def _():
        base_copies[1].start()

    @pl.when(blends)
    def _():
        for i in range(rows_axis - 1):
            side_copy(spots_out, spots_in.at[i], 0).wait_recv()
        for r in range(rows_axis):
            weigh(r)
        for i in range(rows_axis - 1):
            side_copy(base_out.at[pl.ds(0, 1)], base_in.at[i, pl.ds(0, 1)], 1).wait_recv()
        order = [(r, c) for c in early for r in range(rows_axis)]
        order += [(0, c) for c in range(last + 1) if c not in early] + rest
        for r, c in order:
            wait_blocks(r, c)
            blend(r, [0], *chunks[c])
            send_patch(r, 0, *chunks[c])
        for i in range(rows_axis - 1):
            side_copy(
                base_out.at[pl.ds(1, sections - 1)], base_in.at[i, pl.ds(1, sections - 1)], 2
            ).wait_recv()
        for r in range(rows_axis):
            blend(r, list(range(1, sections)), 0, row_count)
            for p in range(1, sections):
                send_patch(r, p, 0, row_count)

    jitter_out[...] = 2.0 * jitter_rows[...].T[0:1, :]
    table_copy.wait()
    down = downward(section, sections)
    done = 0
    for batch in [[0]] + [list(range(i, min(i + 2, sections))) for i in range(1, sections, 2)]:
        order = [i + down * (sections - 1 - 2 * i) for i in batch]
        for s in order:

            @pl.when((section != s) | (row_at != rows_axis - 1))
            def _():
                pltpu.make_async_copy(patch_in.at[s], patch_in.at[s], patch_recv.at[s]).wait()

            @pl.when((section == s) & (row_at == rows_axis - 1))
            def _():
                patch_in[s] = patch_out[(rows_axis - 1) * sections + s]

        spectra = [forward(patch_in[s], tables) for s in order]
        while done < batch[0] - 1:
            pair = done + down * (sections - 2 - 2 * done)
            early_out[pair - down] = surface(freq[pair], freq[pair + 1], tables)
            done += 1
        for s, spectrum in zip(order, spectra):
            freq[s] = spectrum
    last_pair = (1 - down) * (sections - 2)
    freq_out[0] = freq[last_pair]
    freq_out[1] = freq[last_pair + 1]

    @pl.when(me < owners - 1)
    def _():
        halo.wait_send()

    @pl.when(row_at != rows_axis - 1)
    def _():
        pltpu.make_async_copy(outbox, outbox, block_send).wait()
        spots_copy.wait_send()
        for copy in base_copies:
            copy.wait_send()

    @pl.when(blends)
    def _():
        sent = outbox.at[pl.ds(1, tiles - 1)]
        pltpu.make_async_copy(sent, sent, block_send).wait()
        sent = patch_out.at[pl.ds(0, rows_axis * sections - 1)]
        pltpu.make_async_copy(sent, sent, patch_send).wait()


def correlate(sections, freq, tables, jitter, early, jitter_out, surfaces_out, late, sem):
    pairs = early.shape[0]
    down = downward(lax.axis_index("sec"), sections)
    copies = [
        pltpu.make_async_copy(early, surfaces_out.at[pl.ds(down, pairs), 0, 0], sem.at[0]),
        pltpu.make_async_copy(jitter, jitter_out, sem.at[1]),
        pltpu.make_async_copy(late, surfaces_out.at[(1 - down) * pairs, 0, 0], sem.at[2]),
    ]
    copies[0].start()
    copies[1].start()
    late[...] = surface(freq[0], freq[1], tables)
    copies[2].start()
    for copy in copies:
        copy.wait()


def per_device(section_pixels, jitter_index, drift_list, blend_weight, patch_col):
    _, row_count, row_width = section_pixels.shape
    sections = lax.axis_size("sec")
    tiles, rows_axis = lax.axis_size("tile"), lax.axis_size("row")
    owners = tiles * rows_axis
    moves = drift_list.shape[2]
    blocks = row_width // LANES
    chunks = len(row_chunks(row_count))
    pieces = len(load_pieces(row_count))
    sizes = (sections, tiles, rows_axis, row_count, row_width, moves)
    spots = -(-sections // 8) * 8
    tables = dft_tables(PATCH)
    f32, bf16 = jnp.float32, jnp.bfloat16
    vmem = pl.BlockSpec(memory_space=pltpu.VMEM)
    anywhere = pl.BlockSpec(memory_space=pl.ANY)
    dma = pltpu.SemaphoreType.DMA
    between = pl.pallas_call(
        functools.partial(kernel, sizes),
        out_shape=(
            pltpu.VMEM((1, row_count), f32),
            pltpu.VMEM((2, 2 * PATCH, PATCH), f32),
            pltpu.VMEM((sections - 2, PATCH, PATCH), f32),
            pltpu.VMEM(tables.shape, bf16),
        ),
        in_specs=[anywhere] * 6,
        out_specs=(vmem,) * 4,
        scratch_shapes=[
            pltpu.VMEM((row_count, row_width), f32),
            pltpu.VMEM(jitter_index.shape, jnp.int32),
            pltpu.SMEM((1, 3, owners, moves), jnp.int32),
            pltpu.SMEM(blend_weight.shape, f32),
            pltpu.SMEM(patch_col.shape, jnp.int32),
            pltpu.VMEM((row_count, LANES), jnp.int32),
            pltpu.VMEM((blocks + 2, row_count + 8, LANES), f32),
            pltpu.VMEM((blocks, row_count + 8, LANES), f32),
            pltpu.VMEM((row_count, LANES), f32),
            pltpu.VMEM((row_count + 8, LANES), f32),
            pltpu.VMEM((row_count, LANES), f32),
            pltpu.VMEM((blocks, 8, LANES), f32),
            pltpu.VMEM((blocks, 1, LANES), f32),
            pltpu.VMEM((tiles, rows_axis, CAP, BLOCK, BLOCK), bf16),
            pltpu.VMEM((rows_axis, owners - 1, CAP, BLOCK, BLOCK), bf16),
            pltpu.VMEM((spots, LANES), f32),
            pltpu.VMEM((rows_axis - 1, spots, LANES), f32),
            pltpu.VMEM((sections, PATCH, PATCH), bf16),
            pltpu.VMEM((rows_axis - 1, sections, PATCH, PATCH), bf16),
            pltpu.VMEM((rows_axis, sections, owners * CAP + 1, 8, LANES), f32),
            pltpu.VMEM((rows_axis * sections, PATCH, PATCH), bf16),
            pltpu.VMEM((sections, PATCH, PATCH), bf16),
            pltpu.VMEM((sections, 2 * PATCH, PATCH), f32),
            dma((pieces,)),
            dma,
            dma((4,)),
            dma((2,)),
            dma,
            dma((rows_axis, chunks)),
            dma((3,)),
            dma((3,)),
            dma,
            dma((sections,)),
        ],
        compiler_params=pltpu.CompilerParams(collective_id=0, has_side_effects=True),
        name="section_patches",
    )(
        section_pixels,
        jitter_index,
        jnp.transpose(drift_list, (0, 3, 1, 2)),
        blend_weight,
        patch_col,
        tables,
    )
    jitter, freq, early, tables = [
        pltpu.with_memory_space_constraint(x, pltpu.VMEM) for x in between
    ]
    return pl.pallas_call(
        functools.partial(correlate, sections),
        out_shape=(
            jax.ShapeDtypeStruct((1, row_count), f32),
            jax.ShapeDtypeStruct((sections - 1, 1, 1, PATCH, PATCH), f32),
        ),
        in_specs=[vmem] * 4,
        out_specs=(anywhere, anywhere),
        scratch_shapes=[pltpu.VMEM((PATCH, PATCH), f32), dma((3,))],
        name="section_correlation",
    )(freq, tables, jitter, early)


def solution(mesh):
    in_specs = (
        P(("groups", "sec"), ("tile", "row"), None),
        P(("groups", "sec"), ("tile", "row")),
        P(("groups", "sec"), None, None, None),
        P(("groups", "sec"), None, None),
        P(("tile", "row"), "groups"),
    )
    out_specs = (
        P(("groups", "sec"), ("tile", "row")),
        P("groups", ("tile", "row"), "sec", None, None),
    )
    return jax.shard_map(
        per_device, mesh=mesh, in_specs=in_specs, out_specs=out_specs, check_vma=False
    )
```

```python
import functools
import math

import jax
import jax.numpy as jnp
import numpy as np
from jax import lax
from jax.experimental import pallas as pl
from jax.experimental.pallas import tpu as pltpu
from jax.sharding import PartitionSpec as P

SEG = 512
PATCH = 128
BLOCK = 128
CAP = 2
LANES = 128
MESH = pl.DeviceIdType.MESH


def dft_tables(side):
    index = np.arange(side)
    angles = (index[:, None] * index[None, :] % side) * (2.0 * math.pi / side)
    cosine, sine = np.cos(angles), np.sin(angles)
    table = np.concatenate(
        [
            np.concatenate([cosine, sine], 1),
            np.concatenate([cosine, -sine], 1),
            np.concatenate([-sine, -cosine], 1),
        ],
        0,
    )
    high = table.astype(jnp.bfloat16)
    low = (table - high.astype(np.float64)).astype(jnp.bfloat16)
    return np.stack([high, low])


def dot(a, b):
    return jnp.dot(a, b, preferred_element_type=jnp.float32)


def split(a):
    high = a.astype(jnp.bfloat16)
    return high, (a - high.astype(jnp.float32)).astype(jnp.bfloat16)


def dot3(a, b):
    return dot(a[0], b[0]) + (dot(a[0], b[1]) + dot(a[1], b[0]))


def total(terms):
    terms = list(terms)
    while len(terms) > 1:
        terms = [
            terms[i] + terms[i + 1] if i + 1 < len(terms) else terms[i]
            for i in range(0, len(terms), 2)
        ]
    return terms[0]


def take(x, index):
    return jnp.take_along_axis(x, index, axis=1)


def row_chunks(row_count):
    cuts = [0, 16] + list(range(48, row_count - 16, 32)) + [row_count - 16, row_count]
    return [(a, b) for a, b in zip(cuts[:-1], cuts[1:])][::-1]


def load_pieces(row_count):
    cuts = [row_count, row_count - 24, 0]
    return list(zip(cuts[1:], cuts[:-1]))


def downward(section, sections):
    return (section + sections - 1) // sections


def forward(patches, tables):
    wide = tables[0, 0:PATCH, :], tables[1, 0:PATCH, :]
    square = tables[0, PATCH : 3 * PATCH, :], tables[1, PATCH : 3 * PATCH, :]
    values = jnp.concatenate(patches, 0)
    first = dot(values, wide[0]) + dot(values, wide[1])
    stacked = [
        jnp.concatenate([first[at : at + PATCH, :PATCH], first[at : at + PATCH, PATCH:]], 0)
        for at in range(0, len(patches) * PATCH, PATCH)
    ]
    high, low = split(jnp.concatenate(stacked, 1))
    if len(patches) > 1:
        both = dot3(square, (high, low))
        return [both[:, at : at + PATCH] for at in range(0, len(patches) * PATCH, PATCH)]
    both = dot(square[0], jnp.concatenate([high, low], 1))
    return [both[:, :PATCH] + (both[:, PATCH:] + dot(square[1], high))]


def surface(now, after, tables, sign=None):
    wide = tables[0, 0:PATCH, :]
    square = tables[0, PATCH : 3 * PATCH, :]
    now_real, now_imag = now[0:PATCH], now[PATCH : 2 * PATCH]
    next_real, next_imag = after[0:PATCH], after[PATCH : 2 * PATCH]
    cross_real = now_real * next_real + now_imag * next_imag
    cross_imag = now_imag * next_real - now_real * next_imag
    if sign is not None:
        cross_imag = sign * cross_imag
    magnitude = jnp.sqrt(cross_real * cross_real + cross_imag * cross_imag)
    mean = jnp.sum(jnp.sum(magnitude, axis=0, keepdims=True), axis=1, keepdims=True) * (
        1.0 / (PATCH * PATCH)
    )
    scaled = 1.0 / (magnitude + (0.5 * mean + 1e-06))
    damped = jnp.concatenate([cross_real * scaled, cross_imag * scaled], 1)
    back = dot(damped.astype(jnp.bfloat16), square)
    stacked = jnp.concatenate([back[:, :PATCH], back[:, PATCH:]], 0)
    return dot(wide, stacked.astype(jnp.bfloat16)) * (1.0 / PATCH)


def kernel(
    sizes,
    pixels,
    delays_hbm,
    drifts_hbm,
    weights_hbm,
    columns_hbm,
    tables_hbm,
    jitter_out,
    surfaces,
    tables,
    raw,
    delays,
    drifts,
    weights,
    columns,
    delay_rows,
    aligned,
    ahead,
    cross_sums,
    energies,
    jitter_rows,
    halo_out,
    halo_in,
    outbox,
    arrived,
    spots_out,
    spots_in,
    base_out,
    base_in,
    coefs,
    patch_out,
    patch_in,
    freq,
    load_sem,
    table_sem,
    small_sem,
    halo_sem,
    block_send,
    block_recv,
    side_send,
    side_recv,
    patch_send,
    patch_recv,
):
    sections, tiles, rows_axis, row_count, row_width, moves = sizes
    owners = tiles * rows_axis
    blocks = row_width // LANES
    per_seg = SEG // LANES
    segs = row_width // SEG
    slab_blocks = blocks // sections
    chunks = row_chunks(row_count)
    pieces = load_pieces(row_count)
    f32, bf16 = jnp.float32, jnp.bfloat16
    tile, row_at = lax.axis_index("tile"), lax.axis_index("row")
    me = tile * rows_axis + row_at
    section = lax.axis_index("sec")

    def band_device(band):
        return {"tile": band // rows_axis, "row": band % rows_axis}

    last = len(chunks) - 1
    blends = row_at == rows_axis - 1
    others = [i + (i + owners - me) // owners for i in range(owners - 1)]

    def tile_at(step):
        return (tile + step) % tiles

    def blender(at):
        return {"tile": at, "row": rows_axis - 1}

    def place_at(at):
        return me - (me - (at + 1) * rows_axis + owners) // owners

    table_copy = pltpu.make_async_copy(tables_hbm, tables, table_sem)
    loads = [
        pltpu.make_async_copy(
            pixels.at[0, pl.ds(a, b - a)], raw.at[pl.ds(a, b - a)], load_sem.at[i]
        )
        for i, (a, b) in enumerate(pieces)
    ]
    small_copies = [
        pltpu.make_async_copy(source, target, small_sem.at[i])
        for i, (source, target) in enumerate(
            (
                (delays_hbm, delays),
                (drifts_hbm, drifts),
                (weights_hbm, weights),
                (columns_hbm, columns),
            )
        )
    ]
    small_copies[0].start()
    loads[0].start()
    barrier = pltpu.get_barrier_semaphore()
    for step in range(1, sections):
        far = (section + step) % sections
        pl.semaphore_signal(
            barrier, inc=1, device_id={"sec": far, "row": rows_axis - 1}, device_id_type=MESH
        )
    for copy in small_copies[1:] + loads[1:2]:
        copy.start()
    for band in others:
        pl.semaphore_signal(barrier, inc=1, device_id=band_device(band), device_id_type=MESH)

    @pl.when(blends)
    def _():
        for step in range(1, sections):
            for r in range(rows_axis - 1):
                far = {"sec": (section + step) % sections, "row": r}
                pl.semaphore_signal(barrier, inc=1, device_id=far, device_id_type=MESH)

    for copy in loads[2:]:
        copy.start()
    table_copy.start()

    lane = lax.broadcasted_iota(jnp.int32, (8, LANES), 1)
    first_lane, last_lane = lane == 0, lane == LANES - 1
    to_right, to_left = (lane + 1) & (LANES - 1), (lane + LANES - 1) & (LANES - 1)
    zero = jnp.zeros((8, LANES), f32)
    for g in range(0, row_count + 8, 8):
        aligned[0, g : g + 8, :] = zero
        aligned[blocks + 1, g : g + 8, :] = zero
    small_copies[0].wait()
    delay_rows[...] = (
        jnp.broadcast_to(delays[...].astype(f32), (LANES, row_count)).T
    ).astype(jnp.int32)

    def shifted(g):
        start = g * 8
        delay = delay_rows[start : start + 8, :]
        values = [raw[start : start + 8, v * LANES : (v + 1) * LANES] for v in range(blocks)]
        near = lane + delay
        here = [take(x, near & (LANES - 1)) for x in values] + [zero]
        far = near + 1
        there = [take(x, far & (LANES - 1)) for x in values] + [zero]
        near_kept, far_kept = near < LANES, far < LANES
        now, after = [], []
        for v in range(blocks):
            now.append(jnp.where(near_kept, here[v], here[v + 1]))
            x = jnp.where(far_kept, there[v], there[v + 1])
            if v % per_seg == per_seg - 1:
                x = jnp.where(last_lane, there[v + 1 - per_seg], x)
            after.append(x)
        return now, after

    def keep(g, now, after):
        rows = slice(g * 8 + 8, g * 8 + 16)
        for v in range(blocks):
            aligned[v + 1, rows, :] = now[v]
            ahead[v, rows, :] = after[v]
        energies[rows, :] = total(x * x for x in now)

    def compare(g, now=None, after=None):
        start = g * 8
        terms = []
        for v in range(blocks):
            x = now[v] if now else aligned[v + 1, start + 8 : start + 16, :]
            x_after = after[v] if after else ahead[v, start + 8 : start + 16, :]
            above = aligned[v + 1, start + 7 : start + 15, :]
            above_after = ahead[v, start + 7 : start + 15, :]
            terms.append(above * x_after - above_after * x)
        cross_sums[start : start + 8, :] = total(terms)

    halo = pltpu.make_async_remote_copy(
        src_ref=halo_out.at[:, pl.ds(7, 1)],
        dst_ref=halo_in,
        send_sem=halo_sem.at[0],
        recv_sem=halo_sem.at[1],
        device_id=band_device((me + 1) % owners),
        device_id_type=MESH,
    )

    def pick(hits, values, default):
        first = second = default
        for hit, value in zip(hits[::-1], values[::-1]):
            second = jnp.where(hit, first, second)
            first = jnp.where(hit, value, first)
        return first, second

    sources = {}

    def find_sources():
        own_sources = [drifts[0, 0, me, k] for k in range(moves)]
        own_owners = [drifts[0, 1, me, k] for k in range(moves)]
        for step in range(tiles):
            for r in range(rows_axis):
                band = tile_at(step) * rows_axis + r
                picked = pick([o == band for o in own_owners], own_sources, jnp.int32(0))
                for rank in range(CAP):
                    sources[step, r, rank] = picked[rank]

    def corrected(block, start):
        rows = slice(start + 8, start + 16)
        before, x, after = [aligned[block + i, rows, :] for i in range(3)]
        left = take(jnp.where(last_lane, before, x), to_left)
        right = take(jnp.where(first_lane, after, x), to_right)
        return x - jitter_rows[start : start + 8, :] * (right - left)

    def finish(a, b):
        numerator = jnp.sum(cross_sums[a:b, :], axis=1, keepdims=True) * (-0.5 / segs)
        power = energies[a + 8 : b + 8, :] + energies[a + 7 : b + 7, :]
        power = jnp.sum(power, axis=1, keepdims=True) * (0.5 / segs)
        jitter = jnp.broadcast_to(numerator / (power + 1e-05), (b - a, LANES))
        jitter_rows[a:b, :] = 0.5 * jitter

    def fill_blocks(step, r, c):
        a, b = span(r, c)
        for rank in range(CAP):
            for start in range(a, b, 16):
                block = sources[step, r, rank]
                pair = [corrected(block, start + half) for half in (0, 8)]
                outbox[step, r, rank, start : start + 16, :] = jnp.concatenate(pair, 0).astype(bf16)

    def span(r, c):
        return (0, chunks[c][1]) if r and c == last - 1 else chunks[c]

    def landing(r, c):
        return c + r * (last + 1) - max(r - 1, 0)

    def send_blocks(step, sent):
        at = tile_at(step)

        def start():
            for r, c in sent:
                a, b = span(r, c)
                pltpu.make_async_remote_copy(
                    src_ref=outbox.at[step, r, :, pl.ds(a, b - a)],
                    dst_ref=arrived.at[r, place_at(at), :, pl.ds(a, b - a)],
                    send_sem=block_send,
                    recv_sem=block_recv.at[landing(r, c)],
                    device_id=blender(at),
                    device_id_type=MESH,
                ).start()

        if step:
            start()
        else:
            pl.when(row_at != rows_axis - 1)(start)

    def fill_base(patches):
        for p in patches:
            offset = columns[0, p] % LANES
            block = p * slab_blocks + columns[0, p] // LANES
            for start in range(0, row_count, 16):
                pair = []
                for at in (start, start + 8):
                    rows = slice(at + 8, at + 16)
                    before, x, after = [aligned[block + i, rows, :] for i in range(3)]
                    left = jnp.where(lane >= offset - 1, x, after)
                    left = jnp.where((lane - offset) == LANES - 1, before, left)
                    left = take(left, to_left)
                    right = take(jnp.where(lane > offset, x, after), to_right)
                    half = jitter_rows[at : at + 8, :]
                    pair.append(jnp.where(lane >= offset, x, after) - half * (right - left))
                base_out[p, start : start + 16, :] = jnp.concatenate(pair, 0).astype(bf16)

    def side_copy(source, target, i):
        return pltpu.make_async_remote_copy(
            src_ref=source,
            dst_ref=target,
            send_sem=side_send.at[i],
            recv_sem=side_recv.at[i],
            device_id=blender(tile),
            device_id_type=MESH,
        )

    row_slot = row_at % max(rows_axis - 1, 1)
    spots_copy = side_copy(spots_out, spots_in.at[row_slot], 0)
    base_copies = [
        side_copy(base_out.at[pl.ds(0, 1)], base_in.at[row_slot, pl.ds(0, 1)], 1),
        side_copy(
            base_out.at[pl.ds(1, sections - 1)], base_in.at[row_slot, pl.ds(1, sections - 1)], 2
        ),
    ]

    keys = [(i, rank) for i in range(owners) for rank in range(CAP)]

    def spot(r, p):
        spots = spots_out if r == rows_axis - 1 else spots_in.at[r]
        column = jnp.broadcast_to(spots[p : p + 1, :], (8, LANES)).astype(jnp.int32)
        return column & (LANES - 1), p * slab_blocks + column // LANES

    def weigh(r):
        found = {}
        owner = tile * rows_axis + r
        for i, band in enumerate([me] + others):
            hits = [drifts[0, 1, band, k] == owner for k in range(moves)]
            picked = pick(hits, [drifts[0, 2, band, k] for k in range(moves)], jnp.int32(-1))
            heavy = pick(hits, [weights[0, band, k] for k in range(moves)], jnp.float32(0.0))
            for rank in range(CAP):
                found[i, rank] = picked[rank], heavy[rank]
        for p in range(sections):
            first, block = spot(r, p)
            under = jnp.where(lane >= first, block, block + 1)
            shares = [jnp.where(under == found[key][0], found[key][1], 0.0) for key in keys]
            scale = 1.0 / (1.0 + total(shares))
            coefs[r, p, len(keys)] = scale
            for i, share in enumerate(shares):
                coefs[r, p, i] = share * scale

    def wait_blocks(r, c):
        a, b = span(r, c)
        landed = arrived.at[r, :, :, pl.ds(a, b - a)]
        pltpu.make_async_copy(landed, landed, block_recv.at[landing(r, c)]).wait()

    def blend(r, patches, a, b):
        turns = [(lane + spot(r, p)[0]) & (LANES - 1) for p in patches]
        for start in range(a, b, 16):
            rows = slice(start, start + 16)
            moved = [outbox[0, r, rank, rows, :].astype(f32) for rank in range(CAP)]
            moved += [arrived[r, i - 1, rank, rows, :].astype(f32) for i, rank in keys[CAP:]]
            for p, turn in zip(patches, turns):
                base = base_out[p, rows, :] if r == rows_axis - 1 else base_in[r, p, rows, :]
                shares = [coefs[r, p, i] for i in range(len(keys) + 1)]
                values = []
                for i in (0, 8):
                    terms = [share * x[i : i + 8] for share, x in zip(shares, moved)]
                    terms.append(shares[-1] * base[i : i + 8].astype(f32))
                    values.append(take(total(terms), turn))
                patch_out[r * sections + p, rows, :] = jnp.concatenate(values, 0).astype(bf16)

    def send_patch(r, p, a, b):
        @pl.when((section != p) | (r != rows_axis - 1))
        def _():
            pltpu.make_async_remote_copy(
                src_ref=patch_out.at[r * sections + p, pl.ds(a, b - a)],
                dst_ref=patch_in.at[section, pl.ds(a, b - a)],
                send_sem=patch_send,
                recv_sem=patch_recv.at[section],
                device_id={"sec": p, "row": r},
                device_id_type=MESH,
            ).start()

    aligned_groups = set()

    def group(g):
        now, after = shifted(g)
        keep(g, now, after)
        aligned_groups.add(g)
        return now, after

    loaded = 0

    def need(row):
        nonlocal loaded
        while not loaded or pieces[loaded - 1][0] > row:
            loads[loaded].wait()
            loaded += 1

    def groups(c):
        a, b = chunks[c][0] // 8, chunks[c][1] // 8
        for g in range(b - 1, max(a, 1) - 2, -1):
            if g not in aligned_groups:
                need(g * 8)
                group(g)
        for g in range(a, b):
            compare(g)

    def halo_rows():
        rows = [jnp.broadcast_to(halo_in[v], (8, LANES)) for v in range(blocks)]
        turned = [take(x, to_right) for x in rows]
        for v in range(blocks):
            follows = v + 1 - per_seg if v % per_seg == per_seg - 1 else v + 1
            aligned[v + 1, 0:8, :] = rows[v]
            ahead[v, 0:8, :] = jnp.where(last_lane, turned[follows], turned[v])
        energies[0:8, :] = total(x * x for x in rows)

    groups(0)
    for v in range(blocks):
        halo_out[v, :, :] = aligned[v + 1, row_count : row_count + 8, :]
    for copy in small_copies[1:]:
        copy.wait()
    find_sources()
    for p in range(sections):
        spots_out[p : p + 1, :] = jnp.full((1, LANES), columns[0, p]).astype(f32)
    entered = (owners - 1) + (sections - 1) * (1 + (rows_axis - 1) * (row_at // (rows_axis - 1)))
    pl.semaphore_wait(barrier, entered)

    @pl.when(me < owners - 1)
    def _():
        halo.start()

    @pl.when(row_at != rows_axis - 1)
    def _():
        spots_copy.start()

    early = range(last - 1)
    rest = [(r, last - 1) for r in range(1, rows_axis)]
    for c in range(last):
        now = [(r, c) for r in range(rows_axis if c in early else 1)]
        finish(*chunks[c])
        for r, c in now:
            fill_blocks(1, r, c)
        if c == 0:
            send_blocks(1, now)
        if c + 1 < last:
            groups(c + 1)
        else:
            group(0)
        if c:
            send_blocks(1, now)

    @pl.when(me > 0)
    def _():
        halo.wait_recv()

    @pl.when(me == 0)
    def _():
        halo_in[...] = jnp.zeros((blocks, 1, LANES), f32)

    halo_rows()
    for g in range(chunks[last][1] // 8):
        compare(g)
    finish(*chunks[last])
    fill_blocks(1, 0, last)
    send_blocks(1, [(0, last)])
    fill_base([0])

    @pl.when(row_at != rows_axis - 1)
    def _():
        base_copies[0].start()

    def send_all(step, sent):
        for r, c in sent:
            fill_blocks(step, r, c)
        send_blocks(step, sent)

    send_all(0, [(0, c) for c in range(last + 1)])
    send_all(1, rest)
    later = [(r, c) for r in range(1, rows_axis) for c in range(last)]
    send_all(0, later)
    for step in range(2, tiles):
        send_all(step, [(0, c) for c in range(last + 1)] + later)
    fill_base(range(1, sections))

    @pl.when(row_at != rows_axis - 1)
    def _():
        base_copies[1].start()

    @pl.when(blends)
    def _():
        for i in range(rows_axis - 1):
            side_copy(spots_out, spots_in.at[i], 0).wait_recv()
        for r in range(rows_axis):
            weigh(r)
        for i in range(rows_axis - 1):
            side_copy(base_out.at[pl.ds(0, 1)], base_in.at[i, pl.ds(0, 1)], 1).wait_recv()
        order = [(r, c) for c in early for r in range(rows_axis)]
        order += [(0, c) for c in range(last + 1) if c not in early]
        for r, c in order:
            wait_blocks(r, c)
            blend(r, [0], *span(r, c))
            send_patch(r, 0, *span(r, c))
        for i in range(rows_axis - 1):
            side_copy(
                base_out.at[pl.ds(1, sections - 1)], base_in.at[i, pl.ds(1, sections - 1)], 2
            ).wait_recv()
        others_at = list(range(1, sections))
        blend(0, others_at, 0, row_count)

        @pl.when(section == 0)
        def _():
            for p in others_at[::-1]:
                send_patch(0, p, 0, row_count)

        for r, c in rest:
            wait_blocks(r, c)
            blend(r, [0], *span(r, c))
            send_patch(r, 0, *span(r, c))
        for r in range(1, rows_axis):
            blend(r, others_at, 0, row_count)
        for p in others_at:

            @pl.when(section > 0)
            def _():
                send_patch(0, p, 0, row_count)

            for r in range(1, rows_axis):
                send_patch(r, p, 0, row_count)

    jitter_out[...] = 2.0 * jitter_rows[...].T[0:1, :]
    table_copy.wait()
    down = downward(section, sections)
    done = 0
    for batch in [[0]] + [list(range(i, min(i + 2, sections))) for i in range(1, sections, 2)]:
        order = [i + down * (sections - 1 - 2 * i) for i in batch]
        for s in order:

            @pl.when((section != s) | (row_at != rows_axis - 1))
            def _():
                pltpu.make_async_copy(patch_in.at[s], patch_in.at[s], patch_recv.at[s]).wait()

            @pl.when((section == s) & (row_at == rows_axis - 1))
            def _():
                patch_in[s] = patch_out[(rows_axis - 1) * sections + s]

        spectra = forward([patch_in[s] for s in order], tables)
        while done < batch[0] - 1:
            pair = done + down * (sections - 2 - 2 * done)
            surfaces[pair] = surface(freq[pair], freq[pair + 1], tables)
            done += 1
        for i, s, spectrum in zip(batch, order, spectra):
            if i == sections - 1:
                pair = done + down * (sections - 2 - 2 * done)
                sign = (1 - 2 * down).astype(f32)
                surfaces[pair] = surface(freq[pair + down], spectrum, tables, sign)
            else:
                freq[s] = spectrum

    @pl.when(me < owners - 1)
    def _():
        halo.wait_send()

    @pl.when(row_at != rows_axis - 1)
    def _():
        pltpu.make_async_copy(outbox, outbox, block_send).wait()
        spots_copy.wait_send()
        for copy in base_copies:
            copy.wait_send()

    @pl.when(blends)
    def _():
        sent = outbox.at[pl.ds(1, tiles - 1)]
        pltpu.make_async_copy(sent, sent, block_send).wait()
        sent = patch_out.at[pl.ds(0, rows_axis * sections - 1)]
        pltpu.make_async_copy(sent, sent, patch_send).wait()


def deliver(jitter, surfaces, jitter_out, surfaces_out, sem):
    copies = [
        pltpu.make_async_copy(surfaces, surfaces_out.at[:, 0, 0], sem.at[0]),
        pltpu.make_async_copy(jitter, jitter_out, sem.at[1]),
    ]
    for copy in copies:
        copy.start()
    for copy in copies:
        copy.wait()


def per_device(section_pixels, jitter_index, drift_list, blend_weight, patch_col):
    _, row_count, row_width = section_pixels.shape
    sections = lax.axis_size("sec")
    tiles, rows_axis = lax.axis_size("tile"), lax.axis_size("row")
    owners = tiles * rows_axis
    moves = drift_list.shape[2]
    blocks = row_width // LANES
    chunks = len(row_chunks(row_count))
    pieces = len(load_pieces(row_count))
    sizes = (sections, tiles, rows_axis, row_count, row_width, moves)
    spots = -(-sections // 8) * 8
    tables = dft_tables(PATCH)
    f32, bf16 = jnp.float32, jnp.bfloat16
    vmem = pl.BlockSpec(memory_space=pltpu.VMEM)
    anywhere = pl.BlockSpec(memory_space=pl.ANY)
    dma = pltpu.SemaphoreType.DMA
    between = pl.pallas_call(
        functools.partial(kernel, sizes),
        out_shape=(
            pltpu.VMEM((1, row_count), f32),
            pltpu.VMEM((sections - 1, PATCH, PATCH), f32),
        ),
        in_specs=[anywhere] * 6,
        out_specs=(vmem,) * 2,
        scratch_shapes=[
            pltpu.VMEM(tables.shape, bf16),
            pltpu.VMEM((row_count, row_width), f32),
            pltpu.VMEM(jitter_index.shape, jnp.int32),
            pltpu.SMEM((1, 3, owners, moves), jnp.int32),
            pltpu.SMEM(blend_weight.shape, f32),
            pltpu.SMEM(patch_col.shape, jnp.int32),
            pltpu.VMEM((row_count, LANES), jnp.int32),
            pltpu.VMEM((blocks + 2, row_count + 8, LANES), f32),
            pltpu.VMEM((blocks, row_count + 8, LANES), f32),
            pltpu.VMEM((row_count, LANES), f32),
            pltpu.VMEM((row_count + 8, LANES), f32),
            pltpu.VMEM((row_count, LANES), f32),
            pltpu.VMEM((blocks, 8, LANES), f32),
            pltpu.VMEM((blocks, 1, LANES), f32),
            pltpu.VMEM((tiles, rows_axis, CAP, BLOCK, BLOCK), bf16),
            pltpu.VMEM((rows_axis, owners - 1, CAP, BLOCK, BLOCK), bf16),
            pltpu.VMEM((spots, LANES), f32),
            pltpu.VMEM((rows_axis - 1, spots, LANES), f32),
            pltpu.VMEM((sections, PATCH, PATCH), bf16),
            pltpu.VMEM((rows_axis - 1, sections, PATCH, PATCH), bf16),
            pltpu.VMEM((rows_axis, sections, owners * CAP + 1, 8, LANES), f32),
            pltpu.VMEM((rows_axis * sections, PATCH, PATCH), bf16),
            pltpu.VMEM((sections, PATCH, PATCH), bf16),
            pltpu.VMEM((sections, 2 * PATCH, PATCH), f32),
            dma((pieces,)),
            dma,
            dma((4,)),
            dma((2,)),
            dma,
            dma((rows_axis * chunks - (rows_axis - 1),)),
            dma((3,)),
            dma((3,)),
            dma,
            dma((sections,)),
        ],
        compiler_params=pltpu.CompilerParams(collective_id=0, has_side_effects=True),
        name="section_patches",
    )(
        section_pixels,
        jitter_index,
        jnp.transpose(drift_list, (0, 3, 1, 2)),
        blend_weight,
        patch_col,
        tables,
    )
    jitter, surfaces = [pltpu.with_memory_space_constraint(x, pltpu.VMEM) for x in between]
    return pl.pallas_call(
        deliver,
        out_shape=(
            jax.ShapeDtypeStruct((1, row_count), f32),
            jax.ShapeDtypeStruct((sections - 1, 1, 1, PATCH, PATCH), f32),
        ),
        in_specs=[vmem] * 2,
        out_specs=(anywhere, anywhere),
        scratch_shapes=[dma((2,))],
        name="section_surfaces",
    )(jitter, surfaces)


def solution(mesh):
    in_specs = (
        P(("groups", "sec"), ("tile", "row"), None),
        P(("groups", "sec"), ("tile", "row")),
        P(("groups", "sec"), None, None, None),
        P(("groups", "sec"), None, None),
        P(("tile", "row"), "groups"),
    )
    out_specs = (
        P(("groups", "sec"), ("tile", "row")),
        P("groups", ("tile", "row"), "sec", None, None),
    )
    return jax.shard_map(
        per_device, mesh=mesh, in_specs=in_specs, out_specs=out_specs, check_vma=False
    )
```

```python
import functools
import math

import jax
import jax.numpy as jnp
import numpy as np
from jax import lax
from jax.experimental import pallas as pl
from jax.experimental.pallas import tpu as pltpu
from jax.sharding import PartitionSpec as P

SEG = 512
PATCH = 128
BLOCK = 128
CAP = 2
LANES = 128
MESH = pl.DeviceIdType.MESH


def dft_tables(side):
    index = np.arange(side)
    angles = (index[:, None] * index[None, :] % side) * (2.0 * math.pi / side)
    cosine, sine = np.cos(angles), np.sin(angles)
    table = np.concatenate(
        [
            np.concatenate([cosine, sine], 1),
            np.concatenate([cosine, -sine], 1),
            np.concatenate([-sine, -cosine], 1),
        ],
        0,
    )
    high = table.astype(jnp.bfloat16)
    low = (table - high.astype(np.float64)).astype(jnp.bfloat16)
    return np.stack([high, low])


def dot(a, b):
    return jnp.dot(a, b, preferred_element_type=jnp.float32)


def split(a):
    high = a.astype(jnp.bfloat16)
    return high, (a - high.astype(jnp.float32)).astype(jnp.bfloat16)


def dot3(a, b):
    return dot(a[0], b[0]) + (dot(a[0], b[1]) + dot(a[1], b[0]))


def total(terms):
    terms = list(terms)
    while len(terms) > 1:
        terms = [
            terms[i] + terms[i + 1] if i + 1 < len(terms) else terms[i]
            for i in range(0, len(terms), 2)
        ]
    return terms[0]


def take(x, index):
    return jnp.take_along_axis(x, index, axis=1)


def row_chunks(row_count):
    cuts = [0, 16] + list(range(48, row_count - 16, 32)) + [row_count - 16, row_count]
    return [(a, b) for a, b in zip(cuts[:-1], cuts[1:])][::-1]


def load_pieces(row_count):
    cuts = [row_count, row_count - 24, 0]
    return list(zip(cuts[1:], cuts[:-1]))


def downward(section, sections):
    return (section + sections - 1) // sections


def forward(patches, tables):
    wide = tables[0, 0:PATCH, :], tables[1, 0:PATCH, :]
    square = tables[0, PATCH : 3 * PATCH, :], tables[1, PATCH : 3 * PATCH, :]
    values = jnp.concatenate(patches, 0)
    first = dot(values, wide[0]) + dot(values, wide[1])
    stacked = [
        jnp.concatenate([first[at : at + PATCH, :PATCH], first[at : at + PATCH, PATCH:]], 0)
        for at in range(0, len(patches) * PATCH, PATCH)
    ]
    high, low = split(jnp.concatenate(stacked, 1))
    if len(patches) > 1:
        both = dot3(square, (high, low))
        return [both[:, at : at + PATCH] for at in range(0, len(patches) * PATCH, PATCH)]
    both = dot(square[0], jnp.concatenate([high, low], 1))
    return [both[:, :PATCH] + (both[:, PATCH:] + dot(square[1], high))]


def surface(now, after, tables, sign=None):
    wide = tables[0, 0:PATCH, :]
    square = tables[0, PATCH : 3 * PATCH, :]
    now_real, now_imag = now[0:PATCH], now[PATCH : 2 * PATCH]
    next_real, next_imag = after[0:PATCH], after[PATCH : 2 * PATCH]
    cross_real = now_real * next_real + now_imag * next_imag
    cross_imag = now_imag * next_real - now_real * next_imag
    if sign is not None:
        cross_imag = sign * cross_imag
    magnitude = jnp.sqrt(cross_real * cross_real + cross_imag * cross_imag)
    mean = jnp.sum(jnp.sum(magnitude, axis=0, keepdims=True), axis=1, keepdims=True) * (
        1.0 / (PATCH * PATCH)
    )
    scaled = 1.0 / (magnitude + (0.5 * mean + 1e-06))
    damped = jnp.concatenate([cross_real * scaled, cross_imag * scaled], 1)
    back = dot(damped.astype(jnp.bfloat16), square)
    stacked = jnp.concatenate([back[:, :PATCH], back[:, PATCH:]], 0)
    return dot(wide, stacked.astype(jnp.bfloat16)) * (1.0 / PATCH)


def kernel(
    sizes,
    pixels,
    delays_hbm,
    drifts_hbm,
    weights_hbm,
    columns_hbm,
    tables_hbm,
    jitter_out,
    surfaces,
    tables,
    raw,
    delays,
    drifts,
    weights,
    columns,
    delay_rows,
    aligned,
    ahead,
    cross_sums,
    energies,
    jitter_rows,
    halo_out,
    halo_in,
    outbox,
    arrived,
    spots_out,
    spots_in,
    base_out,
    base_in,
    coefs,
    patch_out,
    patch_in,
    freq,
    load_sem,
    table_sem,
    small_sem,
    halo_sem,
    block_send,
    block_recv,
    side_send,
    side_recv,
    patch_send,
    patch_recv,
):
    sections, tiles, rows_axis, row_count, row_width, moves = sizes
    owners = tiles * rows_axis
    blocks = row_width // LANES
    per_seg = SEG // LANES
    segs = row_width // SEG
    slab_blocks = blocks // sections
    chunks = row_chunks(row_count)
    pieces = load_pieces(row_count)
    f32, bf16 = jnp.float32, jnp.bfloat16
    tile, row_at = lax.axis_index("tile"), lax.axis_index("row")
    me = tile * rows_axis + row_at
    section = lax.axis_index("sec")

    def band_device(band):
        return {"tile": band // rows_axis, "row": band % rows_axis}

    last = len(chunks) - 1
    blends = row_at == rows_axis - 1
    others = [i + (i + owners - me) // owners for i in range(owners - 1)]

    def tile_at(step):
        return (tile + step) % tiles

    def blender(at):
        return {"tile": at, "row": rows_axis - 1}

    def place_at(at):
        return me - (me - (at + 1) * rows_axis + owners) // owners

    table_copy = pltpu.make_async_copy(tables_hbm, tables, table_sem)
    loads = [
        pltpu.make_async_copy(
            pixels.at[0, pl.ds(a, b - a)], raw.at[pl.ds(a, b - a)], load_sem.at[i]
        )
        for i, (a, b) in enumerate(pieces)
    ]
    small_copies = [
        pltpu.make_async_copy(source, target, small_sem.at[i])
        for i, (source, target) in enumerate(
            (
                (delays_hbm, delays),
                (drifts_hbm, drifts),
                (weights_hbm, weights),
                (columns_hbm, columns),
            )
        )
    ]
    small_copies[0].start()
    loads[0].start()
    barrier = pltpu.get_barrier_semaphore()
    for step in range(1, sections):
        far = (section + step) % sections
        pl.semaphore_signal(
            barrier, inc=1, device_id={"sec": far, "row": rows_axis - 1}, device_id_type=MESH
        )
    for copy in small_copies[1:] + loads[1:2]:
        copy.start()
    for band in others:
        pl.semaphore_signal(barrier, inc=1, device_id=band_device(band), device_id_type=MESH)

    @pl.when(blends)
    def _():
        for step in range(1, sections):
            for r in range(rows_axis - 1):
                far = {"sec": (section + step) % sections, "row": r}
                pl.semaphore_signal(barrier, inc=1, device_id=far, device_id_type=MESH)

    for copy in loads[2:]:
        copy.start()
    table_copy.start()

    lane = lax.broadcasted_iota(jnp.int32, (8, LANES), 1)
    first_lane, last_lane = lane == 0, lane == LANES - 1
    to_right, to_left = (lane + 1) & (LANES - 1), (lane + LANES - 1) & (LANES - 1)
    zero = jnp.zeros((8, LANES), f32)
    for g in range(0, row_count + 8, 8):
        aligned[0, g : g + 8, :] = zero
        aligned[blocks + 1, g : g + 8, :] = zero
    small_copies[0].wait()
    delay_rows[...] = (
        jnp.broadcast_to(delays[...].astype(f32), (LANES, row_count)).T
    ).astype(jnp.int32)

    def shifted(g):
        start = g * 8
        delay = delay_rows[start : start + 8, :]
        values = [raw[start : start + 8, v * LANES : (v + 1) * LANES] for v in range(blocks)]
        near = lane + delay
        here = [take(x, near & (LANES - 1)) for x in values] + [zero]
        far = near + 1
        there = [take(x, far & (LANES - 1)) for x in values] + [zero]
        near_kept, far_kept = near < LANES, far < LANES
        now, after = [], []
        for v in range(blocks):
            now.append(jnp.where(near_kept, here[v], here[v + 1]))
            x = jnp.where(far_kept, there[v], there[v + 1])
            if v % per_seg == per_seg - 1:
                x = jnp.where(last_lane, there[v + 1 - per_seg], x)
            after.append(x)
        return now, after

    def keep(g, now, after):
        rows = slice(g * 8 + 8, g * 8 + 16)
        for v in range(blocks):
            aligned[v + 1, rows, :] = now[v]
            ahead[v, rows, :] = after[v]
        energies[rows, :] = total(x * x for x in now)

    def compare(g, now=None, after=None):
        start = g * 8
        terms = []
        for v in range(blocks):
            x = now[v] if now else aligned[v + 1, start + 8 : start + 16, :]
            x_after = after[v] if after else ahead[v, start + 8 : start + 16, :]
            above = aligned[v + 1, start + 7 : start + 15, :]
            above_after = ahead[v, start + 7 : start + 15, :]
            terms.append(above * x_after - above_after * x)
        cross_sums[start : start + 8, :] = total(terms)

    halo = pltpu.make_async_remote_copy(
        src_ref=halo_out.at[:, pl.ds(7, 1)],
        dst_ref=halo_in,
        send_sem=halo_sem.at[0],
        recv_sem=halo_sem.at[1],
        device_id=band_device((me + 1) % owners),
        device_id_type=MESH,
    )

    def pick(hits, values, default):
        first = second = default
        for hit, value in zip(hits[::-1], values[::-1]):
            second = jnp.where(hit, first, second)
            first = jnp.where(hit, value, first)
        return first, second

    sources = {}

    def find_sources():
        own_sources = [drifts[0, 0, me, k] for k in range(moves)]
        own_owners = [drifts[0, 1, me, k] for k in range(moves)]
        for step in range(tiles):
            for r in range(rows_axis):
                band = tile_at(step) * rows_axis + r
                picked = pick([o == band for o in own_owners], own_sources, jnp.int32(0))
                for rank in range(CAP):
                    sources[step, r, rank] = picked[rank]

    def corrected(block, start):
        rows = slice(start + 8, start + 16)
        before, x, after = [aligned[block + i, rows, :] for i in range(3)]
        left = take(jnp.where(last_lane, before, x), to_left)
        right = take(jnp.where(first_lane, after, x), to_right)
        return x - jitter_rows[start : start + 8, :] * (right - left)

    def finish(a, b):
        numerator = jnp.sum(cross_sums[a:b, :], axis=1, keepdims=True) * (-0.5 / segs)
        power = energies[a + 8 : b + 8, :] + energies[a + 7 : b + 7, :]
        power = jnp.sum(power, axis=1, keepdims=True) * (0.5 / segs)
        jitter = jnp.broadcast_to(numerator / (power + 1e-05), (b - a, LANES))
        jitter_rows[a:b, :] = 0.5 * jitter

    def fill_blocks(step, r, c):
        a, b = span(r, c)
        for rank in range(CAP):
            for start in range(a, b, 16):
                block = sources[step, r, rank]
                pair = [corrected(block, start + half) for half in (0, 8)]
                outbox[step, r, rank, start : start + 16, :] = jnp.concatenate(pair, 0).astype(bf16)

    def span(r, c):
        return (0, chunks[c][1]) if r and c == last - 1 else chunks[c]

    def landing(r, c):
        return c + r * (last + 1) - max(r - 1, 0)

    def send_blocks(step, sent):
        at = tile_at(step)

        def start():
            for r, c in sent:
                a, b = span(r, c)
                pltpu.make_async_remote_copy(
                    src_ref=outbox.at[step, r, :, pl.ds(a, b - a)],
                    dst_ref=arrived.at[r, place_at(at), :, pl.ds(a, b - a)],
                    send_sem=block_send,
                    recv_sem=block_recv.at[landing(r, c)],
                    device_id=blender(at),
                    device_id_type=MESH,
                ).start()

        if step:
            start()
        else:
            pl.when(row_at != rows_axis - 1)(start)

    def fill_base(patches):
        for p in patches:
            offset = columns[0, p] % LANES
            block = p * slab_blocks + columns[0, p] // LANES
            for start in range(0, row_count, 16):
                pair = []
                for at in (start, start + 8):
                    rows = slice(at + 8, at + 16)
                    before, x, after = [aligned[block + i, rows, :] for i in range(3)]
                    left = jnp.where(lane >= offset - 1, x, after)
                    left = jnp.where((lane - offset) == LANES - 1, before, left)
                    left = take(left, to_left)
                    right = take(jnp.where(lane > offset, x, after), to_right)
                    half = jitter_rows[at : at + 8, :]
                    pair.append(jnp.where(lane >= offset, x, after) - half * (right - left))
                base_out[p, start : start + 16, :] = jnp.concatenate(pair, 0).astype(bf16)

    def side_copy(source, target, i):
        return pltpu.make_async_remote_copy(
            src_ref=source,
            dst_ref=target,
            send_sem=side_send.at[i],
            recv_sem=side_recv.at[i],
            device_id=blender(tile),
            device_id_type=MESH,
        )

    row_slot = row_at % max(rows_axis - 1, 1)
    spots_copy = side_copy(spots_out, spots_in.at[row_slot], 0)
    base_copies = [
        side_copy(base_out.at[pl.ds(0, 1)], base_in.at[row_slot, pl.ds(0, 1)], 1),
        side_copy(
            base_out.at[pl.ds(1, sections - 1)], base_in.at[row_slot, pl.ds(1, sections - 1)], 2
        ),
    ]

    keys = [(i, rank) for i in range(owners) for rank in range(CAP)]

    def spot(r, p):
        spots = spots_out if r == rows_axis - 1 else spots_in.at[r]
        column = jnp.broadcast_to(spots[p : p + 1, :], (8, LANES)).astype(jnp.int32)
        return column & (LANES - 1), p * slab_blocks + column // LANES

    def weigh(r):
        found = {}
        owner = tile * rows_axis + r
        for i, band in enumerate([me] + others):
            hits = [drifts[0, 1, band, k] == owner for k in range(moves)]
            picked = pick(hits, [drifts[0, 2, band, k] for k in range(moves)], jnp.int32(-1))
            heavy = pick(hits, [weights[0, band, k] for k in range(moves)], jnp.float32(0.0))
            for rank in range(CAP):
                found[i, rank] = picked[rank], heavy[rank]
        for p in range(sections):
            first, block = spot(r, p)
            under = jnp.where(lane >= first, block, block + 1)
            shares = [jnp.where(under == found[key][0], found[key][1], 0.0) for key in keys]
            scale = 1.0 / (1.0 + total(shares))
            coefs[r, p, len(keys)] = scale
            for i, share in enumerate(shares):
                coefs[r, p, i] = share * scale

    def wait_blocks(r, c):
        a, b = span(r, c)
        landed = arrived.at[r, :, :, pl.ds(a, b - a)]
        pltpu.make_async_copy(landed, landed, block_recv.at[landing(r, c)]).wait()

    def blend(r, patches, a, b):
        turns = [(lane + spot(r, p)[0]) & (LANES - 1) for p in patches]
        for start in range(a, b, 16):
            rows = slice(start, start + 16)
            moved = [outbox[0, r, rank, rows, :].astype(f32) for rank in range(CAP)]
            moved += [arrived[r, i - 1, rank, rows, :].astype(f32) for i, rank in keys[CAP:]]
            for p, turn in zip(patches, turns):
                base = base_out[p, rows, :] if r == rows_axis - 1 else base_in[r, p, rows, :]
                shares = [coefs[r, p, i] for i in range(len(keys) + 1)]
                values = []
                for i in (0, 8):
                    terms = [share * x[i : i + 8] for share, x in zip(shares, moved)]
                    terms.append(shares[-1] * base[i : i + 8].astype(f32))
                    values.append(take(total(terms), turn))
                patch_out[r * sections + p, rows, :] = jnp.concatenate(values, 0).astype(bf16)

    def send_patch(r, p, a, b):
        @pl.when((section != p) | (r != rows_axis - 1))
        def _():
            pltpu.make_async_remote_copy(
                src_ref=patch_out.at[r * sections + p, pl.ds(a, b - a)],
                dst_ref=patch_in.at[section, pl.ds(a, b - a)],
                send_sem=patch_send,
                recv_sem=patch_recv.at[section],
                device_id={"sec": p, "row": r},
                device_id_type=MESH,
            ).start()

    aligned_groups = set()

    def group(g):
        now, after = shifted(g)
        keep(g, now, after)
        aligned_groups.add(g)
        return now, after

    loaded = 0

    def need(row):
        nonlocal loaded
        while not loaded or pieces[loaded - 1][0] > row:
            loads[loaded].wait()
            loaded += 1

    def groups(c):
        a, b = chunks[c][0] // 8, chunks[c][1] // 8
        for g in range(b - 1, max(a, 1) - 2, -1):
            if g not in aligned_groups:
                need(g * 8)
                group(g)
        for g in range(a, b):
            compare(g)

    def halo_rows():
        rows = [jnp.broadcast_to(halo_in[v], (8, LANES)) for v in range(blocks)]
        turned = [take(x, to_right) for x in rows]
        for v in range(blocks):
            follows = v + 1 - per_seg if v % per_seg == per_seg - 1 else v + 1
            aligned[v + 1, 0:8, :] = rows[v]
            ahead[v, 0:8, :] = jnp.where(last_lane, turned[follows], turned[v])
        energies[0:8, :] = total(x * x for x in rows)

    groups(0)
    for v in range(blocks):
        halo_out[v, :, :] = aligned[v + 1, row_count : row_count + 8, :]
    for copy in small_copies[1:]:
        copy.wait()
    find_sources()
    for p in range(sections):
        spots_out[p : p + 1, :] = jnp.full((1, LANES), columns[0, p]).astype(f32)
    entered = (owners - 1) + (sections - 1) * (1 + (rows_axis - 1) * (row_at // (rows_axis - 1)))
    pl.semaphore_wait(barrier, entered)

    @pl.when(me < owners - 1)
    def _():
        halo.start()

    @pl.when(row_at != rows_axis - 1)
    def _():
        spots_copy.start()

    def send_all(step, sent):
        for r, c in sent:
            fill_blocks(step, r, c)
        send_blocks(step, sent)

    early = range(last - 1)
    rest = [(r, last - 1) for r in range(1, rows_axis)]
    for c in range(last):
        now = [(r, c) for r in range(rows_axis if c in early else 1)]
        finish(*chunks[c])
        send_all(1, now)
        if c + 1 < last:
            groups(c + 1)
        else:
            group(0)

    @pl.when(me > 0)
    def _():
        halo.wait_recv()

    @pl.when(me == 0)
    def _():
        halo_in[...] = jnp.zeros((blocks, 1, LANES), f32)

    halo_rows()
    for g in range(chunks[last][1] // 8):
        compare(g)
    finish(*chunks[last])
    fill_blocks(1, 0, last)
    send_blocks(1, [(0, last)])
    fill_base([0])

    @pl.when(row_at != rows_axis - 1)
    def _():
        base_copies[0].start()

    send_all(0, [(0, c) for c in range(last + 1)])
    send_all(1, rest)
    later = [(r, c) for r in range(1, rows_axis) for c in range(last)]
    send_all(0, later)
    for step in range(2, tiles):
        send_all(step, [(0, c) for c in range(last + 1)] + later)
    fill_base(range(1, sections))

    @pl.when(row_at != rows_axis - 1)
    def _():
        base_copies[1].start()

    @pl.when(blends)
    def _():
        for i in range(rows_axis - 1):
            side_copy(spots_out, spots_in.at[i], 0).wait_recv()
        for r in range(rows_axis):
            weigh(r)
        for i in range(rows_axis - 1):
            side_copy(base_out.at[pl.ds(0, 1)], base_in.at[i, pl.ds(0, 1)], 1).wait_recv()
        order = [(r, c) for c in early for r in range(rows_axis)]
        order += [(0, c) for c in range(last + 1) if c not in early]
        for r, c in order:
            wait_blocks(r, c)
            blend(r, [0], *span(r, c))
            send_patch(r, 0, *span(r, c))
        for i in range(rows_axis - 1):
            side_copy(
                base_out.at[pl.ds(1, sections - 1)], base_in.at[i, pl.ds(1, sections - 1)], 2
            ).wait_recv()
        others_at = list(range(1, sections))
        blend(0, others_at, 0, row_count)

        @pl.when(section == 0)
        def _():
            for p in others_at[::-1]:
                send_patch(0, p, 0, row_count)

        for r, c in rest:
            wait_blocks(r, c)
            blend(r, [0], *span(r, c))
            send_patch(r, 0, *span(r, c))
        for r in range(1, rows_axis):
            blend(r, others_at, 0, row_count)
        for p in others_at:

            @pl.when(section > 0)
            def _():
                send_patch(0, p, 0, row_count)

            for r in range(1, rows_axis):
                send_patch(r, p, 0, row_count)

    jitter_out[...] = 2.0 * jitter_rows[...].T[0:1, :]
    table_copy.wait()
    down = downward(section, sections)
    done = 0
    for batch in [[0]] + [list(range(i, min(i + 2, sections))) for i in range(1, sections, 2)]:
        order = [i + down * (sections - 1 - 2 * i) for i in batch]
        for s in order:

            @pl.when((section != s) | (row_at != rows_axis - 1))
            def _():
                pltpu.make_async_copy(patch_in.at[s], patch_in.at[s], patch_recv.at[s]).wait()

            @pl.when((section == s) & (row_at == rows_axis - 1))
            def _():
                patch_in[s] = patch_out[(rows_axis - 1) * sections + s]

        spectra = forward([patch_in[s] for s in order], tables)
        while done < batch[0] - 1:
            pair = done + down * (sections - 2 - 2 * done)
            surfaces[pair] = surface(freq[pair], freq[pair + 1], tables)
            done += 1
        for i, s, spectrum in zip(batch, order, spectra):
            if i == sections - 1:
                pair = done + down * (sections - 2 - 2 * done)
                sign = (1 - 2 * down).astype(f32)
                surfaces[pair] = surface(freq[pair + down], spectrum, tables, sign)
            else:
                freq[s] = spectrum

    @pl.when(me < owners - 1)
    def _():
        halo.wait_send()

    @pl.when(row_at != rows_axis - 1)
    def _():
        pltpu.make_async_copy(outbox, outbox, block_send).wait()
        spots_copy.wait_send()
        for copy in base_copies:
            copy.wait_send()

    @pl.when(blends)
    def _():
        sent = outbox.at[pl.ds(1, tiles - 1)]
        pltpu.make_async_copy(sent, sent, block_send).wait()
        sent = patch_out.at[pl.ds(0, rows_axis * sections - 1)]
        pltpu.make_async_copy(sent, sent, patch_send).wait()


def deliver(jitter, surfaces, jitter_out, surfaces_out, sem):
    copies = [
        pltpu.make_async_copy(surfaces, surfaces_out.at[:, 0, 0], sem.at[0]),
        pltpu.make_async_copy(jitter, jitter_out, sem.at[1]),
    ]
    for copy in copies:
        copy.start()
    for copy in copies:
        copy.wait()


def per_device(section_pixels, jitter_index, drift_list, blend_weight, patch_col):
    _, row_count, row_width = section_pixels.shape
    sections = lax.axis_size("sec")
    tiles, rows_axis = lax.axis_size("tile"), lax.axis_size("row")
    owners = tiles * rows_axis
    moves = drift_list.shape[2]
    blocks = row_width // LANES
    chunks = len(row_chunks(row_count))
    pieces = len(load_pieces(row_count))
    sizes = (sections, tiles, rows_axis, row_count, row_width, moves)
    spots = -(-sections // 8) * 8
    tables = dft_tables(PATCH)
    f32, bf16 = jnp.float32, jnp.bfloat16
    vmem = pl.BlockSpec(memory_space=pltpu.VMEM)
    anywhere = pl.BlockSpec(memory_space=pl.ANY)
    dma = pltpu.SemaphoreType.DMA
    between = pl.pallas_call(
        functools.partial(kernel, sizes),
        out_shape=(
            pltpu.VMEM((1, row_count), f32),
            pltpu.VMEM((sections - 1, PATCH, PATCH), f32),
        ),
        in_specs=[anywhere] * 6,
        out_specs=(vmem,) * 2,
        scratch_shapes=[
            pltpu.VMEM(tables.shape, bf16),
            pltpu.VMEM((row_count, row_width), f32),
            pltpu.VMEM(jitter_index.shape, jnp.int32),
            pltpu.SMEM((1, 3, owners, moves), jnp.int32),
            pltpu.SMEM(blend_weight.shape, f32),
            pltpu.SMEM(patch_col.shape, jnp.int32),
            pltpu.VMEM((row_count, LANES), jnp.int32),
            pltpu.VMEM((blocks + 2, row_count + 8, LANES), f32),
            pltpu.VMEM((blocks, row_count + 8, LANES), f32),
            pltpu.VMEM((row_count, LANES), f32),
            pltpu.VMEM((row_count + 8, LANES), f32),
            pltpu.VMEM((row_count, LANES), f32),
            pltpu.VMEM((blocks, 8, LANES), f32),
            pltpu.VMEM((blocks, 1, LANES), f32),
            pltpu.VMEM((tiles, rows_axis, CAP, BLOCK, BLOCK), bf16),
            pltpu.VMEM((rows_axis, owners - 1, CAP, BLOCK, BLOCK), bf16),
            pltpu.VMEM((spots, LANES), f32),
            pltpu.VMEM((rows_axis - 1, spots, LANES), f32),
            pltpu.VMEM((sections, PATCH, PATCH), bf16),
            pltpu.VMEM((rows_axis - 1, sections, PATCH, PATCH), bf16),
            pltpu.VMEM((rows_axis, sections, owners * CAP + 1, 8, LANES), f32),
            pltpu.VMEM((rows_axis * sections, PATCH, PATCH), bf16),
            pltpu.VMEM((sections, PATCH, PATCH), bf16),
            pltpu.VMEM((sections, 2 * PATCH, PATCH), f32),
            dma((pieces,)),
            dma,
            dma((4,)),
            dma((2,)),
            dma,
            dma((rows_axis * chunks - (rows_axis - 1),)),
            dma((3,)),
            dma((3,)),
            dma,
            dma((sections,)),
        ],
        compiler_params=pltpu.CompilerParams(collective_id=0, has_side_effects=True),
        name="section_patches",
    )(
        section_pixels,
        jitter_index,
        jnp.transpose(drift_list, (0, 3, 1, 2)),
        blend_weight,
        patch_col,
        tables,
    )
    jitter, surfaces = [pltpu.with_memory_space_constraint(x, pltpu.VMEM) for x in between]
    return pl.pallas_call(
        deliver,
        out_shape=(
            jax.ShapeDtypeStruct((1, row_count), f32),
            jax.ShapeDtypeStruct((sections - 1, 1, 1, PATCH, PATCH), f32),
        ),
        in_specs=[vmem] * 2,
        out_specs=(anywhere, anywhere),
        scratch_shapes=[dma((2,))],
        name="section_surfaces",
    )(jitter, surfaces)


def solution(mesh):
    in_specs = (
        P(("groups", "sec"), ("tile", "row"), None),
        P(("groups", "sec"), ("tile", "row")),
        P(("groups", "sec"), None, None, None),
        P(("groups", "sec"), None, None),
        P(("tile", "row"), "groups"),
    )
    out_specs = (
        P(("groups", "sec"), ("tile", "row")),
        P("groups", ("tile", "row"), "sec", None, None),
    )
    return jax.shard_map(
        per_device, mesh=mesh, in_specs=in_specs, out_specs=out_specs, check_vma=False
    )
```

```python
import functools
import math

import jax
import jax.numpy as jnp
import numpy as np
from jax import lax
from jax.experimental import pallas as pl
from jax.experimental.pallas import tpu as pltpu
from jax.sharding import PartitionSpec as P

SEG = 512
PATCH = 128
BLOCK = 128
CAP = 2
LANES = 128
MESH = pl.DeviceIdType.MESH


def dft_tables(side):
    index = np.arange(side)
    angles = (index[:, None] * index[None, :] % side) * (2.0 * math.pi / side)
    cosine, sine = np.cos(angles), np.sin(angles)
    table = np.concatenate(
        [
            np.concatenate([cosine, sine], 1),
            np.concatenate([cosine, -sine], 1),
            np.concatenate([-sine, -cosine], 1),
        ],
        0,
    )
    high = table.astype(jnp.bfloat16)
    low = (table - high.astype(np.float64)).astype(jnp.bfloat16)
    return np.stack([high, low])


def dot(a, b):
    return jnp.dot(a, b, preferred_element_type=jnp.float32)


def split(a):
    high = a.astype(jnp.bfloat16)
    return high, (a - high.astype(jnp.float32)).astype(jnp.bfloat16)


def dot3(a, b):
    return dot(a[0], b[0]) + (dot(a[0], b[1]) + dot(a[1], b[0]))


def total(terms):
    terms = list(terms)
    while len(terms) > 1:
        terms = [
            terms[i] + terms[i + 1] if i + 1 < len(terms) else terms[i]
            for i in range(0, len(terms), 2)
        ]
    return terms[0]


def take(x, index):
    return jnp.take_along_axis(x, index, axis=1)


def row_chunks(row_count):
    cuts = [0, 16] + list(range(48, row_count - 16, 32)) + [row_count - 16, row_count]
    return [(a, b) for a, b in zip(cuts[:-1], cuts[1:])][::-1]


def load_pieces(row_count):
    cuts = [row_count, row_count - 24, 0]
    return list(zip(cuts[1:], cuts[:-1]))


def downward(section, sections):
    return (section + sections - 1) // sections


def forward(patches, tables):
    wide = tables[0, 0:PATCH, :], tables[1, 0:PATCH, :]
    square = tables[0, PATCH : 3 * PATCH, :], tables[1, PATCH : 3 * PATCH, :]
    values = jnp.concatenate(patches, 0)
    first = dot(values, wide[0]) + dot(values, wide[1])
    stacked = [
        jnp.concatenate([first[at : at + PATCH, :PATCH], first[at : at + PATCH, PATCH:]], 0)
        for at in range(0, len(patches) * PATCH, PATCH)
    ]
    high, low = split(jnp.concatenate(stacked, 1))
    if len(patches) > 1:
        both = dot3(square, (high, low))
        return [both[:, at : at + PATCH] for at in range(0, len(patches) * PATCH, PATCH)]
    both = dot(square[0], jnp.concatenate([high, low], 1))
    return [both[:, :PATCH] + (both[:, PATCH:] + dot(square[1], high))]


def surface(now, after, tables, sign=None):
    wide = tables[0, 0:PATCH, :]
    square = tables[0, PATCH : 3 * PATCH, :]
    now_real, now_imag = now[0:PATCH], now[PATCH : 2 * PATCH]
    next_real, next_imag = after[0:PATCH], after[PATCH : 2 * PATCH]
    cross_real = now_real * next_real + now_imag * next_imag
    cross_imag = now_imag * next_real - now_real * next_imag
    if sign is not None:
        cross_imag = sign * cross_imag
    magnitude = jnp.sqrt(cross_real * cross_real + cross_imag * cross_imag)
    mean = jnp.sum(jnp.sum(magnitude, axis=0, keepdims=True), axis=1, keepdims=True) * (
        1.0 / (PATCH * PATCH)
    )
    scaled = 1.0 / (magnitude + (0.5 * mean + 1e-06))
    damped = jnp.concatenate([cross_real * scaled, cross_imag * scaled], 1)
    back = dot(damped.astype(jnp.bfloat16), square)
    stacked = jnp.concatenate([back[:, :PATCH], back[:, PATCH:]], 0)
    return dot(wide, stacked.astype(jnp.bfloat16)) * (1.0 / PATCH)


def kernel(
    sizes,
    pixels,
    delays_hbm,
    drifts_hbm,
    weights_hbm,
    columns_hbm,
    tables_hbm,
    jitter_out,
    surfaces,
    tables,
    raw,
    delays,
    drifts,
    weights,
    columns,
    delay_rows,
    aligned,
    ahead,
    cross_sums,
    energies,
    jitter_rows,
    halo_out,
    halo_in,
    outbox,
    arrived,
    spots_out,
    spots_in,
    base_out,
    base_in,
    coefs,
    patch_out,
    patch_in,
    freq,
    load_sem,
    table_sem,
    small_sem,
    halo_sem,
    block_send,
    block_recv,
    side_send,
    side_recv,
    patch_send,
    patch_recv,
):
    sections, tiles, rows_axis, row_count, row_width, moves = sizes
    owners = tiles * rows_axis
    blocks = row_width // LANES
    per_seg = SEG // LANES
    segs = row_width // SEG
    slab_blocks = blocks // sections
    chunks = row_chunks(row_count)
    pieces = load_pieces(row_count)
    f32, bf16 = jnp.float32, jnp.bfloat16
    tile, row_at = lax.axis_index("tile"), lax.axis_index("row")
    me = tile * rows_axis + row_at
    section = lax.axis_index("sec")

    def band_device(band):
        return {"tile": band // rows_axis, "row": band % rows_axis}

    last = len(chunks) - 1
    blends = row_at == rows_axis - 1
    others = [i + (i + owners - me) // owners for i in range(owners - 1)]

    def tile_at(step):
        return (tile + step) % tiles

    def blender(at):
        return {"tile": at, "row": rows_axis - 1}

    def place_at(at):
        return me - (me - (at + 1) * rows_axis + owners) // owners

    table_copy = pltpu.make_async_copy(tables_hbm, tables, table_sem)
    loads = [
        pltpu.make_async_copy(
            pixels.at[0, pl.ds(a, b - a)], raw.at[pl.ds(a, b - a)], load_sem.at[i]
        )
        for i, (a, b) in enumerate(pieces)
    ]
    small_copies = [
        pltpu.make_async_copy(source, target, small_sem.at[i])
        for i, (source, target) in enumerate(
            (
                (delays_hbm, delays),
                (drifts_hbm, drifts),
                (weights_hbm, weights),
                (columns_hbm, columns),
            )
        )
    ]
    small_copies[0].start()
    loads[0].start()
    barrier = pltpu.get_barrier_semaphore()
    for step in range(1, sections):
        far = (section + step) % sections
        pl.semaphore_signal(
            barrier, inc=1, device_id={"sec": far, "row": rows_axis - 1}, device_id_type=MESH
        )
    for copy in small_copies[1:] + loads[1:2]:
        copy.start()
    for band in others:
        pl.semaphore_signal(barrier, inc=1, device_id=band_device(band), device_id_type=MESH)

    @pl.when(blends)
    def _():
        for step in range(1, sections):
            for r in range(rows_axis - 1):
                far = {"sec": (section + step) % sections, "row": r}
                pl.semaphore_signal(barrier, inc=1, device_id=far, device_id_type=MESH)

    for copy in loads[2:]:
        copy.start()
    table_copy.start()

    lane = lax.broadcasted_iota(jnp.int32, (8, LANES), 1)
    first_lane, last_lane = lane == 0, lane == LANES - 1
    to_right, to_left = (lane + 1) & (LANES - 1), (lane + LANES - 1) & (LANES - 1)
    zero = jnp.zeros((8, LANES), f32)
    for g in range(0, row_count + 8, 8):
        aligned[0, g : g + 8, :] = zero
        aligned[blocks + 1, g : g + 8, :] = zero
    small_copies[0].wait()
    delay_rows[...] = (
        jnp.broadcast_to(delays[...].astype(f32), (LANES, row_count)).T
    ).astype(jnp.int32)

    def shifted(g):
        start = g * 8
        delay = delay_rows[start : start + 8, :]
        values = [raw[start : start + 8, v * LANES : (v + 1) * LANES] for v in range(blocks)]
        near = lane + delay
        here = [take(x, near & (LANES - 1)) for x in values] + [zero]
        far = near + 1
        there = [take(x, far & (LANES - 1)) for x in values] + [zero]
        near_kept, far_kept = near < LANES, far < LANES
        now, after = [], []
        for v in range(blocks):
            now.append(jnp.where(near_kept, here[v], here[v + 1]))
            x = jnp.where(far_kept, there[v], there[v + 1])
            if v % per_seg == per_seg - 1:
                x = jnp.where(last_lane, there[v + 1 - per_seg], x)
            after.append(x)
        return now, after

    def keep(g, now, after):
        rows = slice(g * 8 + 8, g * 8 + 16)
        for v in range(blocks):
            aligned[v + 1, rows, :] = now[v]
            ahead[v, rows, :] = after[v]
        energies[rows, :] = total(x * x for x in now)

    def compare(g, now=None, after=None):
        start = g * 8
        terms = []
        for v in range(blocks):
            x = now[v] if now else aligned[v + 1, start + 8 : start + 16, :]
            x_after = after[v] if after else ahead[v, start + 8 : start + 16, :]
            above = aligned[v + 1, start + 7 : start + 15, :]
            above_after = ahead[v, start + 7 : start + 15, :]
            terms.append(above * x_after - above_after * x)
        cross_sums[start : start + 8, :] = total(terms)

    halo = pltpu.make_async_remote_copy(
        src_ref=halo_out.at[:, pl.ds(7, 1)],
        dst_ref=halo_in,
        send_sem=halo_sem.at[0],
        recv_sem=halo_sem.at[1],
        device_id=band_device((me + 1) % owners),
        device_id_type=MESH,
    )

    def pick(hits, values, default):
        first = second = default
        for hit, value in zip(hits[::-1], values[::-1]):
            second = jnp.where(hit, first, second)
            first = jnp.where(hit, value, first)
        return first, second

    sources = {}

    def find_sources():
        own_sources = [drifts[0, 0, me, k] for k in range(moves)]
        own_owners = [drifts[0, 1, me, k] for k in range(moves)]
        for step in range(tiles):
            for r in range(rows_axis):
                band = tile_at(step) * rows_axis + r
                picked = pick([o == band for o in own_owners], own_sources, jnp.int32(0))
                for rank in range(CAP):
                    sources[step, r, rank] = picked[rank]

    def corrected(block, start):
        rows = slice(start + 8, start + 16)
        before, x, after = [aligned[block + i, rows, :] for i in range(3)]
        left = take(jnp.where(last_lane, before, x), to_left)
        right = take(jnp.where(first_lane, after, x), to_right)
        return x - jitter_rows[start : start + 8, :] * (right - left)

    def finish(a, b):
        numerator = jnp.sum(cross_sums[a:b, :], axis=1, keepdims=True) * (-0.5 / segs)
        power = energies[a + 8 : b + 8, :] + energies[a + 7 : b + 7, :]
        power = jnp.sum(power, axis=1, keepdims=True) * (0.5 / segs)
        jitter = jnp.broadcast_to(numerator / (power + 1e-05), (b - a, LANES))
        jitter_rows[a:b, :] = 0.5 * jitter

    def fill_blocks(step, r, c):
        a, b = span(r, c)
        for rank in range(CAP):
            for start in range(a, b, 16):
                block = sources[step, r, rank]
                pair = [corrected(block, start + half) for half in (0, 8)]
                outbox[step, r, rank, start : start + 16, :] = jnp.concatenate(pair, 0).astype(bf16)

    def span(r, c):
        return (0, chunks[c][1]) if r and c == last - 1 else chunks[c]

    def landing(r, c):
        return c + r * (last + 1) - max(r - 1, 0)

    def send_blocks(step, sent):
        at = tile_at(step)

        def start():
            for r, c in sent:
                a, b = span(r, c)
                pltpu.make_async_remote_copy(
                    src_ref=outbox.at[step, r, :, pl.ds(a, b - a)],
                    dst_ref=arrived.at[r, place_at(at), :, pl.ds(a, b - a)],
                    send_sem=block_send,
                    recv_sem=block_recv.at[landing(r, c)],
                    device_id=blender(at),
                    device_id_type=MESH,
                ).start()

        if step:
            start()
        else:
            pl.when(row_at != rows_axis - 1)(start)

    def fill_base(patches):
        for p in patches:
            offset = columns[0, p] % LANES
            block = p * slab_blocks + columns[0, p] // LANES
            for start in range(0, row_count, 16):
                pair = []
                for at in (start, start + 8):
                    rows = slice(at + 8, at + 16)
                    before, x, after = [aligned[block + i, rows, :] for i in range(3)]
                    left = jnp.where(lane >= offset - 1, x, after)
                    left = jnp.where((lane - offset) == LANES - 1, before, left)
                    left = take(left, to_left)
                    right = take(jnp.where(lane > offset, x, after), to_right)
                    half = jitter_rows[at : at + 8, :]
                    pair.append(jnp.where(lane >= offset, x, after) - half * (right - left))
                base_out[p, start : start + 16, :] = jnp.concatenate(pair, 0).astype(bf16)

    def side_copy(source, target, i):
        return pltpu.make_async_remote_copy(
            src_ref=source,
            dst_ref=target,
            send_sem=side_send.at[i],
            recv_sem=side_recv.at[i],
            device_id=blender(tile),
            device_id_type=MESH,
        )

    row_slot = row_at % max(rows_axis - 1, 1)
    spots_copy = side_copy(spots_out, spots_in.at[row_slot], 0)
    base_copies = [
        side_copy(base_out.at[pl.ds(0, 1)], base_in.at[row_slot, pl.ds(0, 1)], 1),
        side_copy(
            base_out.at[pl.ds(1, sections - 1)], base_in.at[row_slot, pl.ds(1, sections - 1)], 2
        ),
    ]

    keys = [(i, rank) for i in range(owners) for rank in range(CAP)]

    def spot(r, p):
        spots = spots_out if r == rows_axis - 1 else spots_in.at[r]
        column = jnp.broadcast_to(spots[p : p + 1, :], (8, LANES)).astype(jnp.int32)
        return column & (LANES - 1), p * slab_blocks + column // LANES

    def weigh(r):
        found = {}
        owner = tile * rows_axis + r
        for i, band in enumerate([me] + others):
            hits = [drifts[0, 1, band, k] == owner for k in range(moves)]
            picked = pick(hits, [drifts[0, 2, band, k] for k in range(moves)], jnp.int32(-1))
            heavy = pick(hits, [weights[0, band, k] for k in range(moves)], jnp.float32(0.0))
            for rank in range(CAP):
                found[i, rank] = picked[rank], heavy[rank]
        for p in range(sections):
            first, block = spot(r, p)
            under = jnp.where(lane >= first, block, block + 1)
            shares = [jnp.where(under == found[key][0], found[key][1], 0.0) for key in keys]
            scale = 1.0 / (1.0 + total(shares))
            coefs[r, p, len(keys)] = scale
            for i, share in enumerate(shares):
                coefs[r, p, i] = share * scale

    def wait_blocks(r, c):
        a, b = span(r, c)
        landed = arrived.at[r, :, :, pl.ds(a, b - a)]
        pltpu.make_async_copy(landed, landed, block_recv.at[landing(r, c)]).wait()

    def blend(r, patches, a, b):
        turns = [(lane + spot(r, p)[0]) & (LANES - 1) for p in patches]
        for start in range(a, b, 16):
            rows = slice(start, start + 16)
            moved = [outbox[0, r, rank, rows, :].astype(f32) for rank in range(CAP)]
            moved += [arrived[r, i - 1, rank, rows, :].astype(f32) for i, rank in keys[CAP:]]
            for p, turn in zip(patches, turns):
                base = base_out[p, rows, :] if r == rows_axis - 1 else base_in[r, p, rows, :]
                shares = [coefs[r, p, i] for i in range(len(keys) + 1)]
                values = []
                for i in (0, 8):
                    terms = [share * x[i : i + 8] for share, x in zip(shares, moved)]
                    terms.append(shares[-1] * base[i : i + 8].astype(f32))
                    values.append(take(total(terms), turn))
                patch_out[r * sections + p, rows, :] = jnp.concatenate(values, 0).astype(bf16)

    def send_patch(r, p, a, b):
        @pl.when((section != p) | (r != rows_axis - 1))
        def _():
            pltpu.make_async_remote_copy(
                src_ref=patch_out.at[r * sections + p, pl.ds(a, b - a)],
                dst_ref=patch_in.at[section, pl.ds(a, b - a)],
                send_sem=patch_send,
                recv_sem=patch_recv.at[section],
                device_id={"sec": p, "row": r},
                device_id_type=MESH,
            ).start()

    aligned_groups = set()

    def group(g):
        now, after = shifted(g)
        keep(g, now, after)
        aligned_groups.add(g)
        return now, after

    loaded = 0

    def need(row):
        nonlocal loaded
        while not loaded or pieces[loaded - 1][0] > row:
            loads[loaded].wait()
            loaded += 1

    def groups(c):
        a, b = chunks[c][0] // 8, chunks[c][1] // 8
        for g in range(b - 1, max(a, 1) - 2, -1):
            if g not in aligned_groups:
                need(g * 8)
                group(g)
        for g in range(a, b):
            compare(g)

    def halo_rows():
        rows = [jnp.broadcast_to(halo_in[v], (8, LANES)) for v in range(blocks)]
        turned = [take(x, to_right) for x in rows]
        for v in range(blocks):
            follows = v + 1 - per_seg if v % per_seg == per_seg - 1 else v + 1
            aligned[v + 1, 0:8, :] = rows[v]
            ahead[v, 0:8, :] = jnp.where(last_lane, turned[follows], turned[v])
        energies[0:8, :] = total(x * x for x in rows)

    groups(0)
    for v in range(blocks):
        halo_out[v, :, :] = aligned[v + 1, row_count : row_count + 8, :]
    for copy in small_copies[1:]:
        copy.wait()
    find_sources()
    for p in range(sections):
        spots_out[p : p + 1, :] = jnp.full((1, LANES), columns[0, p]).astype(f32)
    entered = (owners - 1) + (sections - 1) * (1 + (rows_axis - 1) * (row_at // (rows_axis - 1)))
    pl.semaphore_wait(barrier, entered)

    @pl.when(me < owners - 1)
    def _():
        halo.start()

    @pl.when(row_at != rows_axis - 1)
    def _():
        spots_copy.start()

    def send_all(step, sent):
        for r, c in sent:
            fill_blocks(step, r, c)
        send_blocks(step, sent)

    early = range(last - 1)
    rest = [(r, last - 1) for r in range(1, rows_axis)]
    for c in range(last):
        now = [(r, c) for r in range(rows_axis if c in early else 1)]
        finish(*chunks[c])
        send_all(1, now)
        if c + 1 < last:
            groups(c + 1)
        else:
            group(0)

    @pl.when(me > 0)
    def _():
        halo.wait_recv()

    @pl.when(me == 0)
    def _():
        halo_in[...] = jnp.zeros((blocks, 1, LANES), f32)

    halo_rows()
    for g in range(chunks[last][1] // 8):
        compare(g)
    finish(*chunks[last])
    fill_blocks(1, 0, last)
    send_blocks(1, [(0, last)])
    send_all(1, rest)
    fill_base([0])

    @pl.when(row_at != rows_axis - 1)
    def _():
        base_copies[0].start()

    send_all(0, [(0, c) for c in range(last + 1)])
    later = [(r, c) for r in range(1, rows_axis) for c in range(last)]
    send_all(0, later)
    for step in range(2, tiles):
        send_all(step, [(0, c) for c in range(last + 1)] + later)
    fill_base(range(1, sections))

    @pl.when(row_at != rows_axis - 1)
    def _():
        base_copies[1].start()

    @pl.when(blends)
    def _():
        for i in range(rows_axis - 1):
            side_copy(spots_out, spots_in.at[i], 0).wait_recv()
        for r in range(rows_axis):
            weigh(r)
        for i in range(rows_axis - 1):
            side_copy(base_out.at[pl.ds(0, 1)], base_in.at[i, pl.ds(0, 1)], 1).wait_recv()
        order = [(r, c) for c in early for r in range(rows_axis)]
        order += [(0, c) for c in range(last + 1) if c not in early]
        for r, c in order:
            wait_blocks(r, c)
            blend(r, [0], *span(r, c))
            send_patch(r, 0, *span(r, c))
        for i in range(rows_axis - 1):
            side_copy(
                base_out.at[pl.ds(1, sections - 1)], base_in.at[i, pl.ds(1, sections - 1)], 2
            ).wait_recv()
        others_at = list(range(1, sections))
        blend(0, others_at, 0, row_count)

        @pl.when(section == 0)
        def _():
            for p in others_at[::-1]:
                send_patch(0, p, 0, row_count)

        for r, c in rest:
            wait_blocks(r, c)
            blend(r, [0], *span(r, c))
            send_patch(r, 0, *span(r, c))
        for r in range(1, rows_axis):
            blend(r, others_at, 0, row_count)
        for p in others_at:

            @pl.when(section > 0)
            def _():
                send_patch(0, p, 0, row_count)

            for r in range(1, rows_axis):
                send_patch(r, p, 0, row_count)

    jitter_out[...] = 2.0 * jitter_rows[...].T[0:1, :]
    table_copy.wait()
    down = downward(section, sections)
    done = 0
    for batch in [[0]] + [list(range(i, min(i + 2, sections))) for i in range(1, sections, 2)]:
        order = [i + down * (sections - 1 - 2 * i) for i in batch]
        for s in order:

            @pl.when((section != s) | (row_at != rows_axis - 1))
            def _():
                pltpu.make_async_copy(patch_in.at[s], patch_in.at[s], patch_recv.at[s]).wait()

            @pl.when((section == s) & (row_at == rows_axis - 1))
            def _():
                patch_in[s] = patch_out[(rows_axis - 1) * sections + s]

        spectra = forward([patch_in[s] for s in order], tables)
        while done < batch[0] - 1:
            pair = done + down * (sections - 2 - 2 * done)
            surfaces[pair] = surface(freq[pair], freq[pair + 1], tables)
            done += 1
        for i, s, spectrum in zip(batch, order, spectra):
            if i == sections - 1:
                pair = done + down * (sections - 2 - 2 * done)
                sign = (1 - 2 * down).astype(f32)
                surfaces[pair] = surface(freq[pair + down], spectrum, tables, sign)
            else:
                freq[s] = spectrum

    @pl.when(me < owners - 1)
    def _():
        halo.wait_send()

    @pl.when(row_at != rows_axis - 1)
    def _():
        pltpu.make_async_copy(outbox, outbox, block_send).wait()
        spots_copy.wait_send()
        for copy in base_copies:
            copy.wait_send()

    @pl.when(blends)
    def _():
        sent = outbox.at[pl.ds(1, tiles - 1)]
        pltpu.make_async_copy(sent, sent, block_send).wait()
        sent = patch_out.at[pl.ds(0, rows_axis * sections - 1)]
        pltpu.make_async_copy(sent, sent, patch_send).wait()


def deliver(jitter, surfaces, jitter_out, surfaces_out, sem):
    copies = [
        pltpu.make_async_copy(surfaces, surfaces_out.at[:, 0, 0], sem.at[0]),
        pltpu.make_async_copy(jitter, jitter_out, sem.at[1]),
    ]
    for copy in copies:
        copy.start()
    for copy in copies:
        copy.wait()


def per_device(section_pixels, jitter_index, drift_list, blend_weight, patch_col):
    _, row_count, row_width = section_pixels.shape
    sections = lax.axis_size("sec")
    tiles, rows_axis = lax.axis_size("tile"), lax.axis_size("row")
    owners = tiles * rows_axis
    moves = drift_list.shape[2]
    blocks = row_width // LANES
    chunks = len(row_chunks(row_count))
    pieces = len(load_pieces(row_count))
    sizes = (sections, tiles, rows_axis, row_count, row_width, moves)
    spots = -(-sections // 8) * 8
    tables = dft_tables(PATCH)
    f32, bf16 = jnp.float32, jnp.bfloat16
    vmem = pl.BlockSpec(memory_space=pltpu.VMEM)
    anywhere = pl.BlockSpec(memory_space=pl.ANY)
    dma = pltpu.SemaphoreType.DMA
    between = pl.pallas_call(
        functools.partial(kernel, sizes),
        out_shape=(
            pltpu.VMEM((1, row_count), f32),
            pltpu.VMEM((sections - 1, PATCH, PATCH), f32),
        ),
        in_specs=[anywhere] * 6,
        out_specs=(vmem,) * 2,
        scratch_shapes=[
            pltpu.VMEM(tables.shape, bf16),
            pltpu.VMEM((row_count, row_width), f32),
            pltpu.VMEM(jitter_index.shape, jnp.int32),
            pltpu.SMEM((1, 3, owners, moves), jnp.int32),
            pltpu.SMEM(blend_weight.shape, f32),
            pltpu.SMEM(patch_col.shape, jnp.int32),
            pltpu.VMEM((row_count, LANES), jnp.int32),
            pltpu.VMEM((blocks + 2, row_count + 8, LANES), f32),
            pltpu.VMEM((blocks, row_count + 8, LANES), f32),
            pltpu.VMEM((row_count, LANES), f32),
            pltpu.VMEM((row_count + 8, LANES), f32),
            pltpu.VMEM((row_count, LANES), f32),
            pltpu.VMEM((blocks, 8, LANES), f32),
            pltpu.VMEM((blocks, 1, LANES), f32),
            pltpu.VMEM((tiles, rows_axis, CAP, BLOCK, BLOCK), bf16),
            pltpu.VMEM((rows_axis, owners - 1, CAP, BLOCK, BLOCK), bf16),
            pltpu.VMEM((spots, LANES), f32),
            pltpu.VMEM((rows_axis - 1, spots, LANES), f32),
            pltpu.VMEM((sections, PATCH, PATCH), bf16),
            pltpu.VMEM((rows_axis - 1, sections, PATCH, PATCH), bf16),
            pltpu.VMEM((rows_axis, sections, owners * CAP + 1, 8, LANES), f32),
            pltpu.VMEM((rows_axis * sections, PATCH, PATCH), bf16),
            pltpu.VMEM((sections, PATCH, PATCH), bf16),
            pltpu.VMEM((sections, 2 * PATCH, PATCH), f32),
            dma((pieces,)),
            dma,
            dma((4,)),
            dma((2,)),
            dma,
            dma((rows_axis * chunks - (rows_axis - 1),)),
            dma((3,)),
            dma((3,)),
            dma,
            dma((sections,)),
        ],
        compiler_params=pltpu.CompilerParams(collective_id=0, has_side_effects=True),
        name="section_patches",
    )(
        section_pixels,
        jitter_index,
        jnp.transpose(drift_list, (0, 3, 1, 2)),
        blend_weight,
        patch_col,
        tables,
    )
    jitter, surfaces = [pltpu.with_memory_space_constraint(x, pltpu.VMEM) for x in between]
    return pl.pallas_call(
        deliver,
        out_shape=(
            jax.ShapeDtypeStruct((1, row_count), f32),
            jax.ShapeDtypeStruct((sections - 1, 1, 1, PATCH, PATCH), f32),
        ),
        in_specs=[vmem] * 2,
        out_specs=(anywhere, anywhere),
        scratch_shapes=[dma((2,))],
        name="section_surfaces",
    )(jitter, surfaces)


def solution(mesh):
    in_specs = (
        P(("groups", "sec"), ("tile", "row"), None),
        P(("groups", "sec"), ("tile", "row")),
        P(("groups", "sec"), None, None, None),
        P(("groups", "sec"), None, None),
        P(("tile", "row"), "groups"),
    )
    out_specs = (
        P(("groups", "sec"), ("tile", "row")),
        P("groups", ("tile", "row"), "sec", None, None),
    )
    return jax.shard_map(
        per_device, mesh=mesh, in_specs=in_specs, out_specs=out_specs, check_vma=False
    )
```
